32 devices in a mesh: dp: 8 (over z, x), mp: 4 (over y, core).
Axes of the slice: x: 2, y: 2, z: 4, core: 2. Of those that a mesh axis runs over, the one named last changes fastest.
Arguments:
- tokens: bfloat16 [2048, 8192], P('dp', 'mp'), may hold values from -6 to 6
- cotangent: bfloat16 [2048, 8192], P('dp', 'mp'), may hold values from -6 to 6
- w_in: bfloat16 [64, 4, 256, 256], P('mp'), may hold values from -0.1875 to 0.1875
- w_out: bfloat16 [64, 4, 256, 256], P('mp'), may hold values from -0.125 to 0.125
- in_blocks: int32 [64, 4], P('mp'), may hold values from 0 to 31, as said below
- out_blocks: int32 [64, 4], P('mp'), may hold values from 0 to 31, as said below
Outputs:
- output: bfloat16 [2048, 8192], P('dp', 'mp')
- grad_tokens: bfloat16 [2048, 8192], P('dp', 'mp')
- grad_in: float32 [64, 4, 256, 256], P('mp', None, 'dp')
- grad_out: float32 [64, 4, 256, 256], P('mp', None, 'dp')
The draws below stay inside these ranges and needn't reach their ends.
Inputs may be any that keep to these rules, and one draw needn't show every extreme that they name: `in_blocks`: flat butterfly pattern: row j holds p(j mod 32 XOR m) for m = 0, 1, 2, 4, with p a permutation of the 32 input blocks; the 4 entries of a row differ and every block is named by exactly 8 rows. `out_blocks`: the same flat butterfly form with its own permutation q of the 32 output blocks.
All inputs are finite; a program needn't handle non-finite values.
Results may differ from the reference program's by a relative error of at most 0.018.
Values may be sent and summed in bfloat16 or wider, within the bound.
A program may use at most 128 MiB of HBM per device.

```python
import jax
import jax.numpy as jnp
from jax import lax

D = 8192
BS = 256
K = 4
RB = 32
HB = 64
TOKENS = 2048
N_MP = 4


def butterfly_lists(key, salt):
    order = jax.random.permutation(jax.random.fold_in(key, salt), RB).astype(jnp.int32)
    base = jnp.arange(HB, dtype=jnp.int32) % RB
    masks = jnp.array([0, 1, 2, 4], dtype=jnp.int32)
    return order[jnp.bitwise_xor(base[:, None], masks[None, :])].astype(jnp.int32)


def draw_in_blocks(key, part):
    return butterfly_lists(key, 11)


def draw_out_blocks(key, part):
    return butterfly_lists(key, 23)


def block_scale(rng, shape, split, smallest, largest):
    level, own = 1.0, jax.random.fold_in(rng, 6)
    for position, shards_of in split:
        heights = jnp.exp(jax.random.uniform(jax.random.fold_in(own, position), (shards_of,), jnp.float32, smallest / len(split), largest / len(split)))
        level = level * jnp.repeat(heights, shape[position] // shards_of).reshape([-1 if axis == position else 1 for axis in range(len(shape))])
    return level


def gaussian(key, shape, width, limit, pieces=(), held_as=jnp.bfloat16):
    result = width * jax.random.normal(key, shape, jnp.float32)
    if pieces:
        result = result * block_scale(key, shape, pieces, -0.22, 0.18)
    return jnp.clip(result, -limit, limit).astype(held_as)


def setup_inputs(seed: int = 0) -> dict:
    streams_of = jax.random.split(jax.random.key(seed), 7)
    tokens = gaussian(streams_of[0], (TOKENS, D), 1.0, 6.0, ((0, 8), (1, 4)))
    cotangent = gaussian(streams_of[1], (TOKENS, D), 1.0, 6.0, ((0, 8), (1, 4)))
    w_in = gaussian(streams_of[2], (HB, K, BS, BS), (K * BS) ** -0.5, 0.1875, ((0, 4),))
    w_out = gaussian(streams_of[3], (HB, K, BS, BS), (HB * K * BS // RB) ** -0.5, 0.125, ((0, 4),))
    in_blocks = draw_in_blocks(jax.random.fold_in(streams_of[6], 71), 0)
    out_blocks = draw_out_blocks(jax.random.fold_in(streams_of[6], 71), 0)
    return dict(tokens=tokens, cotangent=cotangent, w_in=w_in, w_out=w_out, in_blocks=in_blocks, out_blocks=out_blocks)


def reference(tokens, cotangent, w_in, w_out, in_blocks, out_blocks):
    total = tokens.shape[0]
    group_size = HB // N_MP
    token_blocks = tokens.reshape(total, RB, BS)
    cot_blocks = cotangent.reshape(total, RB, BS)
    w_in_g = w_in.reshape(N_MP, group_size, K, BS, BS)
    w_out_g = w_out.reshape(N_MP, group_size, K, BS, BS)
    in_g = in_blocks.reshape(N_MP, group_size, K).astype(jnp.int32)
    out_g = out_blocks.reshape(N_MP, group_size, K).astype(jnp.int32)

    def group(carry, items):
        out_acc, back_acc = carry
        weight_in, weight_out, idx_in, idx_out = items
        selected = token_blocks[:, idx_in].astype(jnp.float32)
        pre = jnp.einsum('tjkb,jkbc->tjc', selected, weight_in.astype(jnp.float32))
        act = jax.nn.gelu(pre).astype(jnp.bfloat16)
        terms = jnp.einsum('tjb,jkbc->tjkc', act.astype(jnp.float32), weight_out.astype(jnp.float32))
        part = jnp.zeros((total, RB, BS), jnp.float32).at[:, idx_out.reshape(-1)].add(terms.reshape(total, group_size * K, BS))
        part = lax.optimization_barrier(part.reshape(total, D).astype(jnp.bfloat16)).astype(jnp.float32)
        picked = cot_blocks[:, idx_out].astype(jnp.float32)
        d_act = jnp.einsum('tjkc,jkbc->tjb', picked, weight_out.astype(jnp.float32))
        _, pullback = jax.vjp(jax.nn.gelu, pre)
        d_pre = pullback(d_act)[0].astype(jnp.bfloat16)
        grad_o = jnp.einsum('tjb,tjkc->jkbc', act.astype(jnp.float32), picked)
        grad_i = jnp.einsum('tjkb,tjc->jkbc', selected, d_pre.astype(jnp.float32))
        back = jnp.einsum('tjc,jkbc->tjkb', d_pre.astype(jnp.float32), weight_in.astype(jnp.float32))
        back_part = jnp.zeros((total, RB, BS), jnp.float32).at[:, idx_in.reshape(-1)].add(back.reshape(total, group_size * K, BS))
        back_part = lax.optimization_barrier(back_part.reshape(total, D).astype(jnp.bfloat16)).astype(jnp.float32)
        return ((out_acc + part, back_acc + back_part), (grad_i, grad_o))
    start = (jnp.zeros((total, D), jnp.float32), jnp.zeros((total, D), jnp.float32))
    (out_acc, back_acc), (grads_i, grads_o) = lax.scan(group, start, (w_in_g, w_out_g, in_g, out_g))
    scale = 1.0 / jnp.sqrt(jnp.float32(TOKENS))
    grad_in = grads_i.reshape(HB, K, BS, BS) * scale
    grad_out = grads_o.reshape(HB, K, BS, BS) * scale
    return (out_acc.astype(jnp.bfloat16), back_acc.astype(jnp.bfloat16), grad_in, grad_out)
```

```python
import functools
import math

import jax
import jax.numpy as jnp
from jax import lax
from jax.experimental import pallas as pl
from jax.experimental.pallas import tpu as pltpu
from jax.sharding import PartitionSpec as P

MB = 2
MASKS = (0, 1, 2, 4)
MESH = pl.DeviceIdType.MESH
C0 = math.sqrt(2.0 / math.pi)
C1 = 0.044715
GROUP = 8
NQ = 4
BOTH = 0


def place_blocks(values, targets, row_blocks):
    step_tok = values.shape[0]
    side = values.shape[-1]
    flat = values.reshape(step_tok, -1, side)
    placed = (
        jnp.zeros((step_tok, row_blocks, side), jnp.float32).at[:, targets.reshape(-1)].add(flat)
    )
    return placed.reshape(step_tok, row_blocks * side)


def shards_plain(tokens, cotangent, w_in, w_out, in_blocks, out_blocks):
    hb_dev, kk, side, _ = w_in.shape
    total_tok = tokens.shape[0]
    width = tokens.shape[1] * lax.axis_size("mp")
    row_blocks = width // side
    passes = MB
    step_tok = total_tok // passes
    grad_in = jnp.zeros(w_in.shape, jnp.float32)
    grad_out = jnp.zeros(w_out.shape, jnp.float32)
    out_share = None
    outputs = []
    backs = []
    for index in range(passes):
        x_part = tokens[index * step_tok : (index + 1) * step_tok]
        dy_part = cotangent[index * step_tok : (index + 1) * step_tok]
        x_full = lax.all_gather(x_part, "mp", axis=1, tiled=True)
        selected = x_full.reshape(step_tok, row_blocks, side)[:, in_blocks]
        pre = jnp.einsum("tjkb,jkbc->tjc", selected, w_in, preferred_element_type=jnp.float32)
        act = jax.nn.gelu(pre).astype(jnp.bfloat16)
        terms = jnp.einsum("tjb,jkbc->tjkc", act, w_out, preferred_element_type=jnp.float32)
        partial_out = place_blocks(terms, out_blocks, row_blocks)
        outputs.append(
            lax.psum_scatter(
                partial_out.astype(jnp.bfloat16), "mp", scatter_dimension=1, tiled=True
            )
        )
        dy_full = lax.all_gather(dy_part, "mp", axis=1, tiled=True)
        picked = dy_full.reshape(step_tok, row_blocks, side)[:, out_blocks]
        d_act = jnp.einsum("tjkc,jkbc->tjb", picked, w_out, preferred_element_type=jnp.float32)
        _, pullback = jax.vjp(jax.nn.gelu, pre)
        d_pre = pullback(d_act)[0].astype(jnp.bfloat16)
        grad_out = grad_out + jnp.einsum(
            "tjb,tjkc->jkbc", act, picked, preferred_element_type=jnp.float32
        )
        grad_in = grad_in + jnp.einsum(
            "tjkb,tjc->jkbc", selected, d_pre, preferred_element_type=jnp.float32
        )
        back = jnp.einsum("tjc,jkbc->tjkb", d_pre, w_in, preferred_element_type=jnp.float32)
        partial_back = place_blocks(back, in_blocks, row_blocks)
        backs.append(
            lax.psum_scatter(
                partial_back.astype(jnp.bfloat16), "mp", scatter_dimension=1, tiled=True
            )
        )
    scale = 1.0 / math.sqrt(total_tok * lax.axis_size("dp"))
    in_share, out_share = (
        lax.psum_scatter(
            grad_in.astype(jnp.bfloat16), "dp", scatter_dimension=2, tiled=True
        ).astype(jnp.float32),
        lax.psum_scatter(
            grad_out.astype(jnp.bfloat16), "dp", scatter_dimension=2, tiled=True
        ).astype(jnp.float32),
    )
    output = jnp.concatenate(outputs, axis=0)
    grad_tokens = jnp.concatenate(backs, axis=0)
    return (output, grad_tokens, in_share * scale, out_share * scale)


def flip(u, m):
    if m == 0:
        return u
    return u + m * (1 - 2 * ((u // m) % 2))


def dot(a, b, dims):
    return lax.dot_general(a, b, (dims, ((), ())), preferred_element_type=jnp.float32)


def fused_kernel(dims, idx, x_hbm, dy_hbm, win_hbm, wout_hbm, part_out, part_back, red, *scratch):
    ndp, nmp, hb, side, own, tok, rows = dims
    fulls = scratch[:NQ]
    (
        xg, xall, act, dpre, acth, dpreh, mine, theirs, arrived, wbuf, acc, csend, crecv,
        own_sem, y_send, y_recv, c_send, c_recv, f_send, f_recv,
        z_send, z_recv, b_send, b_recv, yf_send, yf_recv, go_sem, w_sem,
        o_send, o_recv, p_send, p_recv, pl_sem, g_send, g_recv, r_send, r_recv, rl_sem,
    ) = scratch[NQ:]
    nz = ndp // 2
    tc = tok // NQ
    nk = len(MASKS)
    dp = lax.axis_index("dp")
    mp = lax.axis_index("mp")
    z, x = dp // 2, dp % 2
    y, core = mp // 2, mp % 2
    other_core = (dp, y * 2 + 1 - core)
    other_y = (dp, (1 - y) * 2 + core)
    other_x = (z * 2 + 1 - x, mp)
    g_core = other_core[1]
    g_y = other_y[1]
    g_far = (1 - y) * 2 + 1 - core
    heavy = core == z // 2
    hbase = (z % 2) * GROUP
    srcs = (x_hbm, dy_hbm)
    parts = (part_out, part_back)

    barrier = pltpu.get_barrier_semaphore()
    peers = [other_core, other_y, other_x] + [((dp + 2 * dz) % ndp, mp) for dz in range(1, nz)]
    for peer in peers:
        pl.semaphore_signal(barrier, inc=1, device_id=peer, device_id_type=MESH)
    pl.semaphore_wait(barrier, len(peers))

    def remote(src, dst, ssem, rsem, peer):
        return pltpu.make_async_remote_copy(
            src_ref=src, dst_ref=dst, send_sem=ssem, recv_sem=rsem,
            device_id=peer, device_id_type=MESH,
        )

    def lanes(i):
        return pl.ds(pl.multiple_of(i * side, side), side)

    def rows_at(base, n):
        return pl.ds(pl.multiple_of(base, n), n)

    def held(a, q, slot):
        return fulls[q].at[a, pl.ds(slot * own, own)]

    def piece(a, q, i):
        return srcs[a].at[pl.ds(q * tc, tc), lanes(i)]

    def to_y(a, q, src, dst):
        return remote(src, dst, y_send.at[a, q], y_recv.at[a, q], other_y)

    def to_core(a, q, src, dst):
        return remote(src, dst, c_send.at[a, q], c_recv.at[a, q], other_core)

    def keep(a, q, src, dst):
        return pltpu.make_async_copy(src, dst, own_sem.at[a, q])

    def landed(send, a, q, slot):
        return send(a, q, held(a, q, slot), held(a, q, slot))

    def forward(a, q, slot):
        return remote(held(a, q, g_y), held(a, q, slot), f_send.at[a, q], f_recv.at[a, q], other_core)

    def w_copies(j, slot):
        return (
            pltpu.make_async_copy(win_hbm.at[j], wbuf.at[slot, 0], w_sem.at[slot, 0, 0]),
            pltpu.make_async_copy(wout_hbm.at[j], wbuf.at[slot, 1], w_sem.at[slot, 1, 0]),
        )

    def loop(n, body, first=0):
        lax.fori_loop(first, n, lambda i, c: (body(i), c)[1], 0)

    for q in range(NQ):
        for a in range(2):
            def start(i, a=a, q=q):
                src, dst = piece(a, q, i), fulls[q].at[a, mp * own + i]
                to_y(a, q, src, dst).start()
                to_core(a, q, src, dst).start()
                keep(a, q, src, dst).start()

            loop(own, start)
    for cp in w_copies(0, 0):
        cp.start()

    def z_rows(zs, q):
        return rows_at(zs * tok + q * tc, tc)

    def z_main(b, zs, q):
        return remote(
            xg.at[y, pl.ds(b * GROUP, GROUP), pl.ds(q * tc, tc)],
            xall.at[y, :, z_rows(zs, q)],
            z_send.at[b, q], z_recv.at[zs, q], ((2 * core + b) * 2 + x, mp),
        )

    def z_both(b, zs, q):
        return remote(
            xg.at[1 - y, pl.ds(b * GROUP, BOTH), pl.ds(q * tc, tc)],
            xall.at[1 - y, pl.ds(0, BOTH), z_rows(zs, q)],
            b_send.at[b, q], b_recv.at[zs, q], ((2 * core + b) * 2 + x, mp),
        )

    def y_forward(a, zs, q):
        part = xall.at[a, pl.ds(BOTH, GROUP - BOTH), z_rows(zs, q)]
        return remote(part, part, yf_send.at[zs, q], yf_recv.at[zs, q], other_y)

    def pass_on(q):
        @pl.when(heavy)
        def _():
            for dz in range(1, nz):
                zs = (z + dz) % nz
                z_main(0, zs, q).wait_recv()
                y_forward(y, zs, q).start()

    for q in range(NQ):
        for a in range(2):
            landed(to_y, a, q, g_y).wait_recv()
            forward(a, q, g_y).start()
        for a in range(2):
            landed(keep, a, q, mp).wait()
            landed(to_core, a, q, g_core).wait_recv()
            forward(a, q, g_far).wait_recv()

        def pack(i, q=q):
            for a in range(2):
                xg[a, i, pl.ds(q * tc, tc)] = fulls[q][a, idx[a, i]]

        loop(hb, pack)
        for b in range(2):
            @pl.when(2 * core + b != z)
            def _(b=b, q=q):
                z_main(b, z, q).start()
                if BOTH:
                    z_both(b, z, q).start()

        @pl.when(heavy)
        def _(q=q):
            def own_rows(r):
                for a in range(2):
                    xall[a, r, z_rows(z, q)] = xg[a, hbase + r, pl.ds(q * tc, tc)]

            loop(GROUP, own_rows)

        if q:
            pass_on(q - 1)

    def hidden_math(source_in, source_out, slot):
        pre = dot(source_in(0), wbuf[slot, 0, 0], ((1,), (0,)))
        d_act = dot(source_out(0), wbuf[slot, 1, 0], ((1,), (1,)))
        for k in range(1, nk):
            pre += dot(source_in(k), wbuf[slot, 0, k], ((1,), (0,)))
            d_act += dot(source_out(k), wbuf[slot, 1, k], ((1,), (1,)))
        th = jnp.tanh(C0 * (pre + C1 * (pre * pre * pre)))
        half = 0.5 * (1.0 + th)
        slope = half + 0.5 * pre * (1.0 - th * th) * (C0 * (1.0 + 3.0 * C1 * pre * pre))
        return (pre * half).astype(jnp.bfloat16), (d_act * slope).astype(jnp.bfloat16)

    def hidden(j):
        slot = j % 2
        for cp in w_copies(j, slot):
            cp.wait()

        @pl.when(j + 1 < hb)
        def _():
            for cp in w_copies(j + 1, 1 - slot):
                cp.start()

        act[j], dpre[j] = hidden_math(
            lambda k: xg[0, flip(j, MASKS[k])], lambda k: xg[1, flip(j, MASKS[k])], slot
        )

    loop(hb, hidden)
    pass_on(NQ - 1)

    def v_copies(u, slot):
        res = []
        for k, m in enumerate(MASKS):
            v = flip(u, m)
            res.append(pltpu.make_async_copy(win_hbm.at[v, k], wbuf.at[slot, 0, k], w_sem.at[slot, 0, k]))
            res.append(pltpu.make_async_copy(wout_hbm.at[v, k], wbuf.at[slot, 1, k], w_sem.at[slot, 1, k]))
        return res

    for cp in v_copies(0, 0):
        cp.start()

    @pl.when(heavy)
    def _():
        def own_hidden(r):
            acth[r, rows_at(z * tok, tok)] = act[hbase + r]
            dpreh[r, rows_at(z * tok, tok)] = dpre[hbase + r]

        loop(GROUP, own_hidden)

    def place(u):
        slot = u % 2
        for cp in v_copies(u, slot):
            cp.wait()

        @pl.when(u + 1 < hb)
        def _():
            for cp in v_copies(u + 1, 1 - slot):
                cp.start()

        out = jnp.zeros((tok, side), jnp.float32)
        back = jnp.zeros((tok, side), jnp.float32)
        for k, m in enumerate(MASKS):
            v = flip(u, m)
            out += dot(act[v], wbuf[slot, 1, k], ((1,), (0,)))
            back += dot(dpre[v], wbuf[slot, 0, k], ((1,), (1,)))
        acc[0, u] = out.astype(jnp.bfloat16)
        acc[1, u] = back.astype(jnp.bfloat16)

    loop(hb, place)
    for a in range(2):
        acc[a, hb] = jnp.zeros((tok, side), jnp.bfloat16)

    @pl.when(heavy)
    def _():
        for cp in w_copies(hbase, 0):
            cp.start()

    tables = (1, 0)

    def swap(a):
        return remote(csend.at[a], crecv.at[a], o_send.at[a], o_recv.at[a], other_core)

    for a in range(2):
        for yy in range(2):
            def fill(i, a=a, yy=yy):
                csend[a, yy, i] = acc[a, idx[tables[a], hb + (2 * yy + 1 - core) * own + i]]
            loop(own, fill)
        swap(a).start()

    def to_part(a, i):
        return remote(
            crecv.at[a, 1 - y, i], parts[a].at[1, :, lanes(i)], p_send.at[a, i], p_recv.at[a, i], other_y
        )

    def keep_part(a, i):
        return pltpu.make_async_copy(crecv.at[a, y, i], parts[a].at[0, :, lanes(i)], pl_sem.at[a, i])

    for a in range(2):
        swap(a).wait_recv()
        for yy in range(2):
            def join(i, a=a, yy=yy):
                crecv[a, yy, i] = crecv[a, yy, i] + acc[a, idx[tables[a], hb + (2 * yy + core) * own + i]]
            loop(own, join)

    @pl.when(heavy)
    def _():
        for q in range(NQ):
            for dz in range(1, nz):
                zs = (z + dz) % nz
                y_forward(1 - y, zs, q).wait_recv()
                if BOTH:
                    z_both(0, zs, q).wait_recv()
        pl.semaphore_signal(go_sem, inc=1, device_id=other_core, device_id_type=MESH)

    @pl.when(jnp.logical_not(heavy))
    def _():
        pl.semaphore_wait(go_sem, 1)

    for a in range(2):
        def emit(i, a=a):
            to_part(a, i).start()
            keep_part(a, i).start()
        loop(own, emit)

    def to_x(r):
        return remote(theirs.at[r], arrived.at[r], g_send.at[r], g_recv.at[r], other_x)

    def to_z(r, zd, b, zs):
        return remote(
            mine.at[r, :, :, zd], red.at[:, b * GROUP + r],
            r_send.at[r, zd], r_recv.at[b, r], (zd * 2 + x, mp),
        )

    def keep_z(r):
        return pltpu.make_async_copy(mine.at[r, :, :, z], red.at[:, hbase + r], rl_sem.at[r])

    def settle(r):
        to_x(r).wait_recv()
        for a in range(2):
            for k in range(nk):
                mine[r, a, k] = (
                    mine[r, a, k].astype(jnp.float32) + arrived[r, a, k].astype(jnp.float32)
                ).astype(jnp.bfloat16)
        for dz in (2, 1, 3):
            to_z(r, (z + dz) % nz, z % 2, z).start()
        keep_z(r).start()

    @pl.when(heavy)
    def _():
        def near_hidden(r):
            slot = r % 2
            for cp in w_copies(hbase + r, slot):
                cp.wait()

            @pl.when(r + 1 < GROUP)
            def _():
                for cp in w_copies(hbase + r + 1, 1 - slot):
                    cp.start()

            def one(dz):
                at = rows_at(((z + dz) % nz) * tok, tok)
                acth[r, at], dpreh[r, at] = hidden_math(
                    lambda k: xall[0, flip(r, MASKS[k]), at], lambda k: xall[1, flip(r, MASKS[k]), at], slot
                )

            loop(nz, one, 1)

        loop(GROUP, near_hidden)

        def grads(r):
            for k, m in enumerate(MASKS):
                gi = dot(xall[0, flip(r, m)], dpreh[r], ((0,), (0,)))
                go = dot(acth[r], xall[1, flip(r, m)], ((0,), (0,)))
                for a, value in ((0, gi), (1, go)):
                    value = value.astype(jnp.bfloat16).reshape(nz, 2, rows, side)
                    low, high = value[:, 0], value[:, 1]
                    mine[r, a, k] = jnp.where(x == 0, low, high)
                    theirs[r, a, k] = jnp.where(x == 0, high, low)
            to_x(r).start()

            @pl.when(r > 0)
            def _():
                settle(r - 1)

        loop(GROUP, grads)
        settle(GROUP - 1)

    for q in range(NQ):
        for a in range(2):
            landed(to_y, a, q, mp).wait_send()
            landed(to_core, a, q, mp).wait_send()
            forward(a, q, g_y).wait_send()
        for b in range(2):
            @pl.when(2 * core + b != z)
            def _(b=b, q=q):
                z_main(b, z, q).wait_send()
                if BOTH:
                    z_both(b, z, q).wait_send()

        @pl.when(heavy)
        def _(q=q):
            for dz in range(1, nz):
                y_forward(y, (z + dz) % nz, q).wait_send()
    for a in range(2):
        def drain(i, a=a):
            to_part(a, i).wait_send()
            to_part(a, i).wait_recv()
            keep_part(a, i).wait()
        loop(own, drain)
        swap(a).wait_send()

    @pl.when(heavy)
    def _():
        def sent(r):
            to_x(r).wait_send()
            keep_z(r).wait()
            for dz in range(1, nz):
                to_z(r, (z + dz) % nz, 0, z).wait_send()

        loop(GROUP, sent)

    for b in range(2):
        @pl.when(2 * core + b != z)
        def _(b=b):
            def got(r):
                to_z(r, z, b, z).wait_recv()

            loop(GROUP, got)


def shards_fused(ndp, nmp, tokens, cotangent, w_in, w_out, in_blocks, out_blocks):
    hb, kk, side, _ = w_in.shape
    tok, feats = tokens.shape
    own = feats // side
    blocks = own * nmp
    nz = ndp // 2
    rows = side // ndp
    tc = tok // NQ
    first = jnp.stack([in_blocks[:, 0], out_blocks[:, 0]])
    place = jnp.arange(hb, dtype=jnp.int32)[:, None]
    hit = first[:, :, None] == jnp.arange(blocks, dtype=jnp.int32)
    table = jnp.concatenate([first, jnp.min(jnp.where(hit, place, hb), axis=1)], axis=1)
    bf = jnp.bfloat16
    any_spec = pl.BlockSpec(memory_space=pl.ANY)
    smem = pl.BlockSpec(memory_space=pltpu.SMEM)
    dma = pltpu.SemaphoreType.DMA
    part_out, part_back, red = pl.pallas_call(
        functools.partial(fused_kernel, (ndp, nmp, hb, side, own, tok, rows)),
        out_shape=(
            jax.ShapeDtypeStruct((2, tok, feats), bf),
            jax.ShapeDtypeStruct((2, tok, feats), bf),
            jax.ShapeDtypeStruct((2, hb, kk, rows, side), bf),
        ),
        in_specs=[smem] + [any_spec] * 4,
        out_specs=(any_spec,) * 3,
        scratch_shapes=[pltpu.VMEM((2, blocks, tc, side), bf)] * NQ
        + [
            pltpu.VMEM((2, hb, tok, side), bf),
            pltpu.VMEM((2, GROUP, nz * tok, side), bf),
            pltpu.VMEM((hb, tok, side), bf),
            pltpu.VMEM((hb, tok, side), bf),
            pltpu.VMEM((GROUP, nz * tok, side), bf),
            pltpu.VMEM((GROUP, nz * tok, side), bf),
            pltpu.VMEM((GROUP, 2, kk, nz, rows, side), bf),
            pltpu.VMEM((GROUP, 2, kk, nz, rows, side), bf),
            pltpu.VMEM((GROUP, 2, kk, nz, rows, side), bf),
            pltpu.VMEM((2, 2, kk, side, side), bf),
            pltpu.VMEM((2, hb + 1, tok, side), bf),
            pltpu.VMEM((2, 2, own, tok, side), bf),
            pltpu.VMEM((2, 2, own, tok, side), bf),
        ]
        + [dma((2, NQ))] * 7
        + [dma((2, NQ)), dma((nz, NQ))] * 2
        + [dma((nz, NQ))] * 2
        + [pltpu.SemaphoreType.REGULAR, dma((2, 2, kk))]
        + [dma((2,))] * 2
        + [dma((2, own))] * 3
        + [dma((GROUP,))] * 2
        + [dma((GROUP, nz)), dma((2, GROUP)), dma((GROUP,))],
        compiler_params=pltpu.CompilerParams(
            collective_id=0, has_side_effects=True, vmem_limit_bytes=67_000_000
        ),
    )(
        table,
        tokens, cotangent, w_in, w_out,
    )
    scale = 1.0 / math.sqrt(tok * ndp)
    wide = jnp.float32

    def both(part):
        return (part[0].astype(wide) + part[1].astype(wide)).astype(bf)

    return both(part_out), both(part_back), red[0].astype(wide) * scale, red[1].astype(wide) * scale


def solution(mesh):
    ndp, nmp = mesh.shape["dp"], mesh.shape["mp"]

    def shards(tokens, cotangent, w_in, w_out, in_blocks, out_blocks):
        hb, kk, side, _ = w_in.shape
        blocks = tokens.shape[1] * nmp // side
        fits = (
            nmp == 4
            and kk == len(MASKS)
            and ndp == 2 * nmp
            and blocks == GROUP * nmp
            and 2 * hb == blocks
            and tokens.shape[0] % (16 * NQ) == 0
            and side % (16 * ndp) == 0
        )
        args = (tokens, cotangent, w_in, w_out, in_blocks, out_blocks)
        if fits:
            return shards_fused(ndp, nmp, *args)
        return shards_plain(*args)

    placed = (
        P("dp", "mp"),
        P("dp", "mp"),
        P("mp", None, None, None),
        P("mp", None, None, None),
        P("mp", None),
        P("mp", None),
    )
    return jax.shard_map(
        shards,
        mesh=mesh,
        in_specs=placed,
        out_specs=(
            P("dp", "mp"),
            P("dp", "mp"),
            P("mp", None, "dp", None),
            P("mp", None, "dp", None),
        ),
        check_vma=False,
    )
```

```python
import functools
import math

import jax
import jax.numpy as jnp
from jax import lax
from jax.experimental import pallas as pl
from jax.experimental.pallas import tpu as pltpu
from jax.sharding import PartitionSpec as P

MB = 2
MASKS = (0, 1, 2, 4)
MESH = pl.DeviceIdType.MESH
C0 = math.sqrt(2.0 / math.pi)
C1 = 0.044715
GROUP = 8
NQ = 4
BOTH = 2
SLOTS = 4


def place_blocks(values, targets, row_blocks):
    step_tok = values.shape[0]
    side = values.shape[-1]
    flat = values.reshape(step_tok, -1, side)
    placed = (
        jnp.zeros((step_tok, row_blocks, side), jnp.float32).at[:, targets.reshape(-1)].add(flat)
    )
    return placed.reshape(step_tok, row_blocks * side)


def shards_plain(tokens, cotangent, w_in, w_out, in_blocks, out_blocks):
    hb_dev, kk, side, _ = w_in.shape
    total_tok = tokens.shape[0]
    width = tokens.shape[1] * lax.axis_size("mp")
    row_blocks = width // side
    passes = MB
    step_tok = total_tok // passes
    grad_in = jnp.zeros(w_in.shape, jnp.float32)
    grad_out = jnp.zeros(w_out.shape, jnp.float32)
    out_share = None
    outputs = []
    backs = []
    for index in range(passes):
        x_part = tokens[index * step_tok : (index + 1) * step_tok]
        dy_part = cotangent[index * step_tok : (index + 1) * step_tok]
        x_full = lax.all_gather(x_part, "mp", axis=1, tiled=True)
        selected = x_full.reshape(step_tok, row_blocks, side)[:, in_blocks]
        pre = jnp.einsum("tjkb,jkbc->tjc", selected, w_in, preferred_element_type=jnp.float32)
        act = jax.nn.gelu(pre).astype(jnp.bfloat16)
        terms = jnp.einsum("tjb,jkbc->tjkc", act, w_out, preferred_element_type=jnp.float32)
        partial_out = place_blocks(terms, out_blocks, row_blocks)
        outputs.append(
            lax.psum_scatter(
                partial_out.astype(jnp.bfloat16), "mp", scatter_dimension=1, tiled=True
            )
        )
        dy_full = lax.all_gather(dy_part, "mp", axis=1, tiled=True)
        picked = dy_full.reshape(step_tok, row_blocks, side)[:, out_blocks]
        d_act = jnp.einsum("tjkc,jkbc->tjb", picked, w_out, preferred_element_type=jnp.float32)
        _, pullback = jax.vjp(jax.nn.gelu, pre)
        d_pre = pullback(d_act)[0].astype(jnp.bfloat16)
        grad_out = grad_out + jnp.einsum(
            "tjb,tjkc->jkbc", act, picked, preferred_element_type=jnp.float32
        )
        grad_in = grad_in + jnp.einsum(
            "tjkb,tjc->jkbc", selected, d_pre, preferred_element_type=jnp.float32
        )
        back = jnp.einsum("tjc,jkbc->tjkb", d_pre, w_in, preferred_element_type=jnp.float32)
        partial_back = place_blocks(back, in_blocks, row_blocks)
        backs.append(
            lax.psum_scatter(
                partial_back.astype(jnp.bfloat16), "mp", scatter_dimension=1, tiled=True
            )
        )
    scale = 1.0 / math.sqrt(total_tok * lax.axis_size("dp"))
    in_share, out_share = (
        lax.psum_scatter(
            grad_in.astype(jnp.bfloat16), "dp", scatter_dimension=2, tiled=True
        ).astype(jnp.float32),
        lax.psum_scatter(
            grad_out.astype(jnp.bfloat16), "dp", scatter_dimension=2, tiled=True
        ).astype(jnp.float32),
    )
    output = jnp.concatenate(outputs, axis=0)
    grad_tokens = jnp.concatenate(backs, axis=0)
    return (output, grad_tokens, in_share * scale, out_share * scale)


def flip(u, m):
    if m == 0:
        return u
    return u + m * (1 - 2 * ((u // m) % 2))


def dot(a, b, dims):
    return lax.dot_general(a, b, (dims, ((), ())), preferred_element_type=jnp.float32)


def fused_kernel(dims, idx, x_hbm, dy_hbm, win_hbm, wout_hbm, part_out, part_back, red, *scratch):
    ndp, nmp, hb, side, own, tok, rows = dims
    fulls = [scratch[a * NQ : (a + 1) * NQ] for a in range(2)]
    (
        xg, xall, act, dpre, acth, dpreh, mine, theirs, arrived, wall, crecv,
        own_sem, y_send, y_recv, c_send, c_recv, f_send, f_recv, z_send, b_send, z_recv, b_recv,
        yf_send, yf_recv, go_sem, w_sem,
        o_send, o_recv, p_send, p_recv, pl_sem, g_send, g_recv, r_send, r_recv, rl_sem,
    ) = scratch[2 * NQ :]
    nz = ndp // 2
    tc = tok // NQ
    blocks = own * nmp
    dp = lax.axis_index("dp")
    mp = lax.axis_index("mp")
    z, x = dp // 2, dp % 2
    y, core = mp // 2, mp % 2
    other_core = (dp, y * 2 + 1 - core)
    other_y = (dp, (1 - y) * 2 + core)
    other_x = (z * 2 + 1 - x, mp)
    g_core = other_core[1]
    g_y = other_y[1]
    g_far = (1 - y) * 2 + 1 - core
    heavy = core == z // 2
    hbase = (z % 2) * GROUP
    srcs = (x_hbm, dy_hbm)
    parts = (part_out, part_back)

    barrier = pltpu.get_barrier_semaphore()
    peers = [other_core, other_y, other_x] + [((dp + 2 * dz) % ndp, mp) for dz in range(1, nz)]
    for peer in peers:
        pl.semaphore_signal(barrier, inc=1, device_id=peer, device_id_type=MESH)
    pl.semaphore_wait(barrier, len(peers))

    def remote(src, dst, ssem, rsem, peer):
        return pltpu.make_async_remote_copy(
            src_ref=src, dst_ref=dst, send_sem=ssem, recv_sem=rsem,
            device_id=peer, device_id_type=MESH,
        )

    def lanes(i):
        return pl.ds(pl.multiple_of(i * side, side), side)

    def rows_at(base, n):
        return pl.ds(pl.multiple_of(base, tc), n)

    def held(a, q, slot):
        return fulls[a][q].at[pl.ds(slot * own, own)]

    def piece(a, q, i):
        return srcs[a].at[pl.ds(q * tc, tc), lanes(i)]

    def to_y(a, q, src, dst):
        return remote(src, dst, y_send.at[a, q], y_recv.at[a, q], other_y)

    def to_core(a, q, src, dst):
        return remote(src, dst, c_send.at[a, q], c_recv.at[a, q], other_core)

    def keep(a, q, src, dst):
        return pltpu.make_async_copy(src, dst, own_sem.at[a, q])

    def landed(send, a, q, slot):
        return send(a, q, held(a, q, slot), held(a, q, slot))

    def forward(a, q, slot):
        return remote(held(a, q, g_y), held(a, q, slot), f_send.at[a, q], f_recv.at[a, q], other_core)

    def weights(j):
        return (
            pltpu.make_async_copy(win_hbm.at[j], wall.at[0, j], w_sem.at[0, j]),
            pltpu.make_async_copy(wout_hbm.at[j], wall.at[1, j], w_sem.at[1, j]),
        )

    def loop(n, body, first=0):
        lax.fori_loop(first, n, lambda i, c: (body(i), c)[1], 0)

    for first in (True, False):
        for q in range(NQ):
            for a in range(2):
                def start(i, a=a, q=q):
                    src, dst = piece(a, q, i), fulls[a][q].at[mp * own + i]
                    to_y(a, q, src, dst).start()
                    to_core(a, q, src, dst).start()
                    keep(a, q, src, dst).start()

                @pl.when((y != a) if first else (y == a))
                def _(start=start):
                    loop(own, start)

    def fetch(j):
        for cp in weights(j):
            cp.start()

    loop(hb, fetch)

    def z_rows(slot, q):
        return rows_at((q * nz + slot) * tc, tc)

    def z_main(b, slot, q):
        return remote(
            xg.at[y, pl.ds(b * GROUP, GROUP), pl.ds(q * tc, tc)],
            xall.at[y, :, z_rows(slot, q)],
            z_send.at[b, q], z_recv.at[slot, q], ((2 * core + b) * 2 + x, mp),
        )

    def z_both(b, slot, q):
        return remote(
            xg.at[1 - y, pl.ds(b * GROUP, BOTH), pl.ds(q * tc, tc)],
            xall.at[1 - y, pl.ds(0, BOTH), z_rows(slot, q)],
            b_send.at[b, q], b_recv.at[slot, q], ((2 * core + b) * 2 + x, mp),
        )

    def y_forward(a, slot, q):
        part = xall.at[a, pl.ds(BOTH, GROUP - BOTH), z_rows(slot, q)]
        return remote(part, part, yf_send.at[slot, q], yf_recv.at[slot, q], other_y)

    def to_groups(send, q):
        for b in range(2):
            @pl.when(2 * core + b != z)
            def _(b=b):
                send(b, (z - 2 * core - b + nz) % nz, q).start()

    def pass_on(q):
        @pl.when(heavy)
        def _():
            for slot in range(1, nz):
                z_main(0, slot, q).wait_recv()
                y_forward(y, slot, q).start()

    def gather(a, q):
        landed(to_y, a, q, g_y).wait_recv()
        forward(a, q, g_y).start()
        landed(keep, a, q, mp).wait()
        landed(to_core, a, q, g_core).wait_recv()
        forward(a, q, g_far).wait_recv()

        def pack(i):
            xg[a, i, pl.ds(q * tc, tc)] = fulls[a][q][idx[a, i]]

        loop(hb, pack)

        @pl.when(heavy)
        def _():
            def own_rows(r):
                xall[a, r, z_rows(0, q)] = xg[a, hbase + r, pl.ds(q * tc, tc)]

            loop(GROUP, own_rows)

    def hidden_math(xs, dys, j):
        wi = wall[0, j].reshape(len(MASKS) * side, side)
        wo = jnp.concatenate([wall[1, j, k] for k in range(len(MASKS))], axis=1)
        pre = dot(jnp.concatenate(xs, axis=1), wi, ((1,), (0,)))
        d_act = dot(jnp.concatenate(dys, axis=1), wo, ((1,), (1,)))
        sq = pre * pre
        th = jnp.tanh(pre * (C0 + (C0 * C1) * sq))
        half = 0.5 + 0.5 * th
        value = pre * half
        slope = half + value * (1.0 - th) * (C0 + (3.0 * C0 * C1) * sq)
        return value.astype(jnp.bfloat16), (d_act * slope).astype(jnp.bfloat16)

    def hidden(q):
        at = pl.ds(q * tc, tc)

        def one(j):
            if q == 0:
                for cp in weights(j):
                    cp.wait()
            act[j, at], dpre[j, at] = hidden_math(
                [xg[0, flip(j, m), at] for m in MASKS], [xg[1, flip(j, m), at] for m in MASKS], j
            )

        loop(hb, one)

    for q in range(NQ):
        for a in range(2):
            @pl.when(y == a)
            def _(a=a, q=q):
                gather(a, q)

        to_groups(z_main, q)
    for q in range(NQ):
        for a in range(2):
            @pl.when(y != a)
            def _(a=a, q=q):
                gather(a, q)

        if BOTH:
            to_groups(z_both, q)
        if q:
            pass_on(q - 1)
        hidden(q)
    pass_on(NQ - 1)

    for q in range(NQ):
        for a in range(2):
            forward(a, q, g_y).wait_send()
            fulls[a][q][blocks] = jnp.zeros((tc, side), jnp.bfloat16)

    def place(u):
        vs = [flip(u, m) for m in MASKS]
        wo = jnp.concatenate([wall[1, v, k] for k, v in enumerate(vs)], axis=0)
        wi = jnp.concatenate([wall[0, v, k] for k, v in enumerate(vs)], axis=1)
        out = dot(jnp.concatenate([act[v] for v in vs], axis=1), wo, ((1,), (0,)))
        back = dot(jnp.concatenate([dpre[v] for v in vs], axis=1), wi, ((1,), (1,)))
        for a, value in ((0, out), (1, back)):
            value = value.astype(jnp.bfloat16)
            for q in range(NQ):
                fulls[a][q][u] = value[q * tc : (q + 1) * tc]

    loop(hb, place)
    tables = (1, 0)

    def swap(a, q):
        return remote(
            fulls[a][q].at[pl.ds(hb, hb)], crecv.at[a, :, pl.ds(q * tc, tc)],
            o_send.at[a, q], o_recv.at[a, q], other_core,
        )

    for a in range(2):
        for q in range(NQ):
            for yy in range(2):
                def fill(i, a=a, yy=yy, q=q):
                    fulls[a][q][hb + yy * own + i] = fulls[a][q][
                        idx[tables[a], hb + (2 * yy + 1 - core) * own + i]
                    ]
                loop(own, fill)
            swap(a, q).start()

    def to_part(a, i):
        return remote(
            crecv.at[a, (1 - y) * own + i], parts[a].at[1, :, lanes(i)],
            p_send.at[a, i], p_recv.at[a, i], other_y,
        )

    def keep_part(a, i):
        return pltpu.make_async_copy(
            crecv.at[a, y * own + i], parts[a].at[0, :, lanes(i)], pl_sem.at[a, i]
        )

    for a in range(2):
        for q in range(NQ):
            swap(a, q).wait_recv()
            at = pl.ds(q * tc, tc)
            for yy in range(2):
                def join(i, a=a, yy=yy, q=q, at=at):
                    crecv[a, yy * own + i, at] = crecv[a, yy * own + i, at] + fulls[a][q][
                        idx[tables[a], hb + (2 * yy + core) * own + i]
                    ]
                loop(own, join)

    def near(q):
        for slot in range(1, nz):
            y_forward(1 - y, slot, q).wait_recv()
            if BOTH:
                z_both(0, slot, q).wait_recv()
        at = pl.ds((q * nz + 1) * tc, (nz - 1) * tc)

        def one(r):
            acth[r, at], dpreh[r, at] = hidden_math(
                [xall[0, flip(r, m), at] for m in MASKS], [xall[1, flip(r, m), at] for m in MASKS], hbase + r
            )

        loop(GROUP, one)

    @pl.when(heavy)
    def _():
        def own_hidden(r):
            for q in range(NQ):
                acth[r, z_rows(0, q)] = act[hbase + r, pl.ds(q * tc, tc)]
                dpreh[r, z_rows(0, q)] = dpre[hbase + r, pl.ds(q * tc, tc)]

        loop(GROUP, own_hidden)
        for q in range(NQ):
            near(q)
        pl.semaphore_signal(go_sem, inc=1, device_id=other_core, device_id_type=MESH)

    @pl.when(jnp.logical_not(heavy))
    def _():
        pl.semaphore_wait(go_sem, 1)

    for a in range(2):
        def emit(i, a=a):
            to_part(a, i).start()
            keep_part(a, i).start()
        loop(own, emit)

    def to_x(r, a):
        return remote(
            theirs.at[r % SLOTS, a], arrived.at[r, a], g_send.at[r, a], g_recv.at[r, a], other_x
        )

    def to_z(r, a, zd, b):
        return remote(
            mine.at[r, a, :, zd], red.at[a, b * GROUP + r],
            r_send.at[r, a, zd], r_recv.at[b, r, a], (zd * 2 + x, mp),
        )

    def keep_z(r, a):
        return pltpu.make_async_copy(mine.at[r, a, :, z], red.at[a, hbase + r], rl_sem.at[r, a])

    def settle(r, a):
        to_x(r, a).wait_recv()
        mine[r, a] = (
            mine[r, a].astype(jnp.float32) + arrived[r, a].astype(jnp.float32)
        ).astype(jnp.bfloat16)
        for dz in (2, 1, 3):
            to_z(r, a, (z + dz) % nz, z % 2).start()
        keep_z(r, a).start()

    @pl.when(heavy)
    def _():
        def grads(r):
            for a in range(2):
                @pl.when(r >= SLOTS)
                def _(a=a):
                    to_x(r - SLOTS, a).wait_send()

                for k, m in enumerate(MASKS):
                    if a == 0:
                        value = dot(xall[0, flip(r, m)], dpreh[r], ((0,), (0,)))
                    else:
                        value = dot(acth[r], xall[1, flip(r, m)], ((0,), (0,)))
                    value = value.astype(jnp.bfloat16).reshape(nz, 2, rows, side)
                    low, high = value[:, 0], value[:, 1]
                    mine[r, a, k] = jnp.where(x == 0, low, high)
                    theirs[r % SLOTS, a, k] = jnp.where(x == 0, high, low)
                to_x(r, a).start()
                if a == 0:
                    @pl.when(r > 0)
                    def _():
                        settle(r - 1, 1)
                else:
                    settle(r, 0)

        loop(GROUP, grads)
        settle(GROUP - 1, 1)

    for q in range(NQ):
        for a in range(2):
            landed(to_y, a, q, mp).wait_send()
            landed(to_core, a, q, mp).wait_send()
            swap(a, q).wait_send()
        for b in range(2):
            @pl.when(2 * core + b != z)
            def _(b=b, q=q):
                z_main(b, 0, q).wait_send()
                if BOTH:
                    z_both(b, 0, q).wait_send()

        @pl.when(heavy)
        def _(q=q):
            for slot in range(1, nz):
                y_forward(y, slot, q).wait_send()
    for a in range(2):
        def drain(i, a=a):
            to_part(a, i).wait_send()
            to_part(a, i).wait_recv()
            keep_part(a, i).wait()
        loop(own, drain)

    @pl.when(heavy)
    def _():
        def sent(r):
            for a in range(2):
                @pl.when(r >= GROUP - SLOTS)
                def _(a=a):
                    to_x(r, a).wait_send()

                keep_z(r, a).wait()
                for dz in range(1, nz):
                    to_z(r, a, (z + dz) % nz, 0).wait_send()

        loop(GROUP, sent)

    for b in range(2):
        @pl.when(2 * core + b != z)
        def _(b=b):
            def got(r):
                for a in range(2):
                    to_z(r, a, z, b).wait_recv()

            loop(GROUP, got)


def shards_fused(ndp, nmp, tokens, cotangent, w_in, w_out, in_blocks, out_blocks):
    hb, kk, side, _ = w_in.shape
    tok, feats = tokens.shape
    own = feats // side
    blocks = own * nmp
    nz = ndp // 2
    rows = side // ndp
    tc = tok // NQ
    first = jnp.stack([in_blocks[:, 0], out_blocks[:, 0]])
    place = jnp.arange(hb, dtype=jnp.int32)[:, None]
    hit = first[:, :, None] == jnp.arange(blocks, dtype=jnp.int32)
    table = jnp.concatenate([first, jnp.min(jnp.where(hit, place, blocks), axis=1)], axis=1)
    bf = jnp.bfloat16
    any_spec = pl.BlockSpec(memory_space=pl.ANY)
    smem = pl.BlockSpec(memory_space=pltpu.SMEM)
    dma = pltpu.SemaphoreType.DMA
    part_out, part_back, red = pl.pallas_call(
        functools.partial(fused_kernel, (ndp, nmp, hb, side, own, tok, rows)),
        out_shape=(
            jax.ShapeDtypeStruct((2, tok, feats), bf),
            jax.ShapeDtypeStruct((2, tok, feats), bf),
            jax.ShapeDtypeStruct((2, hb, kk, rows, side), bf),
        ),
        in_specs=[smem] + [any_spec] * 4,
        out_specs=(any_spec,) * 3,
        scratch_shapes=[pltpu.VMEM((blocks + 1, tc, side), bf)] * (2 * NQ)
        + [
            pltpu.VMEM((2, hb, tok, side), bf),
            pltpu.VMEM((2, GROUP, nz * tok, side), bf),
            pltpu.VMEM((hb, tok, side), bf),
            pltpu.VMEM((hb, tok, side), bf),
            pltpu.VMEM((GROUP, nz * tok, side), bf),
            pltpu.VMEM((GROUP, nz * tok, side), bf),
            pltpu.VMEM((GROUP, 2, kk, nz, rows, side), bf),
            pltpu.VMEM((SLOTS, 2, kk, nz, rows, side), bf),
            pltpu.VMEM((GROUP, 2, kk, nz, rows, side), bf),
            pltpu.VMEM((2, hb, kk, side, side), bf),
            pltpu.VMEM((2, hb, tok, side), bf),
        ]
        + [dma((2, NQ))] * 9
        + [dma((nz, NQ))] * 4
        + [pltpu.SemaphoreType.REGULAR, dma((2, hb))]
        + [dma((2, NQ))] * 2
        + [dma((2, own))] * 3
        + [dma((GROUP, 2))] * 2
        + [dma((GROUP, 2, nz)), dma((2, GROUP, 2)), dma((GROUP, 2))],
        compiler_params=pltpu.CompilerParams(
            collective_id=0, has_side_effects=True, vmem_limit_bytes=67_000_000
        ),
    )(
        table,
        tokens, cotangent, w_in, w_out,
    )
    scale = 1.0 / math.sqrt(tok * ndp)
    wide = jnp.float32

    def both(part):
        return (part[0].astype(wide) + part[1].astype(wide)).astype(bf)

    return both(part_out), both(part_back), red[0].astype(wide) * scale, red[1].astype(wide) * scale


def solution(mesh):
    ndp, nmp = mesh.shape["dp"], mesh.shape["mp"]

    def shards(tokens, cotangent, w_in, w_out, in_blocks, out_blocks):
        hb, kk, side, _ = w_in.shape
        blocks = tokens.shape[1] * nmp // side
        fits = (
            nmp == 4
            and kk == len(MASKS)
            and ndp == 2 * nmp
            and blocks == GROUP * nmp
            and 2 * hb == blocks
            and tokens.shape[0] % (16 * NQ) == 0
            and side % (16 * ndp) == 0
        )
        args = (tokens, cotangent, w_in, w_out, in_blocks, out_blocks)
        if fits:
            return shards_fused(ndp, nmp, *args)
        return shards_plain(*args)

    placed = (
        P("dp", "mp"),
        P("dp", "mp"),
        P("mp", None, None, None),
        P("mp", None, None, None),
        P("mp", None),
        P("mp", None),
    )
    return jax.shard_map(
        shards,
        mesh=mesh,
        in_specs=placed,
        out_specs=(
            P("dp", "mp"),
            P("dp", "mp"),
            P("mp", None, "dp", None),
            P("mp", None, "dp", None),
        ),
        check_vma=False,
    )
```

```python
import functools
import math

import jax
import jax.numpy as jnp
from jax import lax
from jax.experimental import pallas as pl
from jax.experimental.pallas import tpu as pltpu
from jax.sharding import PartitionSpec as P

MB = 2
MASKS = (0, 1, 2, 4)
MESH = pl.DeviceIdType.MESH
C0 = math.sqrt(2.0 / math.pi)
C1 = 0.044715
GROUP = 8
NQ = 4
BOTHS = (3, 3, 2, 2)
SLOTS = 4
HALVES = 2


def place_blocks(values, targets, row_blocks):
    step_tok = values.shape[0]
    side = values.shape[-1]
    flat = values.reshape(step_tok, -1, side)
    placed = (
        jnp.zeros((step_tok, row_blocks, side), jnp.float32).at[:, targets.reshape(-1)].add(flat)
    )
    return placed.reshape(step_tok, row_blocks * side)


def shards_plain(tokens, cotangent, w_in, w_out, in_blocks, out_blocks):
    hb_dev, kk, side, _ = w_in.shape
    total_tok = tokens.shape[0]
    width = tokens.shape[1] * lax.axis_size("mp")
    row_blocks = width // side
    passes = MB
    step_tok = total_tok // passes
    grad_in = jnp.zeros(w_in.shape, jnp.float32)
    grad_out = jnp.zeros(w_out.shape, jnp.float32)
    out_share = None
    outputs = []
    backs = []
    for index in range(passes):
        x_part = tokens[index * step_tok : (index + 1) * step_tok]
        dy_part = cotangent[index * step_tok : (index + 1) * step_tok]
        x_full = lax.all_gather(x_part, "mp", axis=1, tiled=True)
        selected = x_full.reshape(step_tok, row_blocks, side)[:, in_blocks]
        pre = jnp.einsum("tjkb,jkbc->tjc", selected, w_in, preferred_element_type=jnp.float32)
        act = jax.nn.gelu(pre).astype(jnp.bfloat16)
        terms = jnp.einsum("tjb,jkbc->tjkc", act, w_out, preferred_element_type=jnp.float32)
        partial_out = place_blocks(terms, out_blocks, row_blocks)
        outputs.append(
            lax.psum_scatter(
                partial_out.astype(jnp.bfloat16), "mp", scatter_dimension=1, tiled=True
            )
        )
        dy_full = lax.all_gather(dy_part, "mp", axis=1, tiled=True)
        picked = dy_full.reshape(step_tok, row_blocks, side)[:, out_blocks]
        d_act = jnp.einsum("tjkc,jkbc->tjb", picked, w_out, preferred_element_type=jnp.float32)
        _, pullback = jax.vjp(jax.nn.gelu, pre)
        d_pre = pullback(d_act)[0].astype(jnp.bfloat16)
        grad_out = grad_out + jnp.einsum(
            "tjb,tjkc->jkbc", act, picked, preferred_element_type=jnp.float32
        )
        grad_in = grad_in + jnp.einsum(
            "tjkb,tjc->jkbc", selected, d_pre, preferred_element_type=jnp.float32
        )
        back = jnp.einsum("tjc,jkbc->tjkb", d_pre, w_in, preferred_element_type=jnp.float32)
        partial_back = place_blocks(back, in_blocks, row_blocks)
        backs.append(
            lax.psum_scatter(
                partial_back.astype(jnp.bfloat16), "mp", scatter_dimension=1, tiled=True
            )
        )
    scale = 1.0 / math.sqrt(total_tok * lax.axis_size("dp"))
    in_share, out_share = (
        lax.psum_scatter(
            grad_in.astype(jnp.bfloat16), "dp", scatter_dimension=2, tiled=True
        ).astype(jnp.float32),
        lax.psum_scatter(
            grad_out.astype(jnp.bfloat16), "dp", scatter_dimension=2, tiled=True
        ).astype(jnp.float32),
    )
    output = jnp.concatenate(outputs, axis=0)
    grad_tokens = jnp.concatenate(backs, axis=0)
    return (output, grad_tokens, in_share * scale, out_share * scale)


def flip(u, m):
    if m == 0:
        return u
    return u + m * (1 - 2 * ((u // m) % 2))


def dot(a, b, dims):
    return lax.dot_general(a, b, (dims, ((), ())), preferred_element_type=jnp.float32)


def fused_kernel(dims, idx, x_hbm, dy_hbm, win_hbm, wout_hbm, out_hbm, back_hbm, red, *scratch):
    ndp, nmp, hb, side, own, tok, rows = dims
    fulls = [scratch[a * NQ : (a + 1) * NQ] for a in range(2)]
    (
        xg, xall, act, dpre, acth, dpreh, mine, theirs, arrived, wall, crecv,
        own_sem, y_send, y_recv, c_send, c_recv, f_send, f_recv, z_send, b_send, z_recv, b_recv,
        yf_send, yf_recv, go_sem, w_sem,
        free_sem, o_send, o_recv, p_send, p_recv, out_sem, g_send, g_recv, r_send, r_recv, rl_sem,
    ) = scratch[2 * NQ :]
    nz = ndp // 2
    tc = tok // NQ
    blocks = own * nmp
    dp = lax.axis_index("dp")
    mp = lax.axis_index("mp")
    z, x = dp // 2, dp % 2
    y, core = mp // 2, mp % 2
    other_core = (dp, y * 2 + 1 - core)
    other_y = (dp, (1 - y) * 2 + core)
    other_x = (z * 2 + 1 - x, mp)
    g_core = other_core[1]
    g_y = other_y[1]
    g_far = (1 - y) * 2 + 1 - core
    heavy = core == z // 2
    hbase = (z % 2) * GROUP
    srcs = (x_hbm, dy_hbm)
    outs = (out_hbm, back_hbm)

    barrier = pltpu.get_barrier_semaphore()
    peers = [other_core, other_y, other_x] + [((dp + 2 * dz) % ndp, mp) for dz in range(1, nz)]
    for peer in peers:
        pl.semaphore_signal(barrier, inc=1, device_id=peer, device_id_type=MESH)
    pl.semaphore_wait(barrier, len(peers))

    def remote(src, dst, ssem, rsem, peer):
        return pltpu.make_async_remote_copy(
            src_ref=src, dst_ref=dst, send_sem=ssem, recv_sem=rsem,
            device_id=peer, device_id_type=MESH,
        )

    def lanes(i):
        return pl.ds(pl.multiple_of(i * side, side), side)

    def rows_at(base, n):
        return pl.ds(pl.multiple_of(base, tc), n)

    def held(a, q, slot):
        return fulls[a][q].at[pl.ds(slot * own, own)]

    def piece(a, q, i):
        return srcs[a].at[pl.ds(q * tc, tc), lanes(i)]

    def to_y(a, q, src, dst):
        return remote(src, dst, y_send.at[a, q], y_recv.at[a, q], other_y)

    def to_core(a, q, src, dst):
        return remote(src, dst, c_send.at[a, q], c_recv.at[a, q], other_core)

    def keep(a, q, src, dst):
        return pltpu.make_async_copy(src, dst, own_sem.at[a, q])

    def landed(send, a, q, slot):
        return send(a, q, held(a, q, slot), held(a, q, slot))

    def forward(a, q, slot):
        return remote(held(a, q, g_y), held(a, q, slot), f_send.at[a, q], f_recv.at[a, q], other_core)

    def weights():
        return (
            pltpu.make_async_copy(win_hbm, wall.at[0], w_sem.at[0]),
            pltpu.make_async_copy(wout_hbm, wall.at[1], w_sem.at[1]),
        )

    def loop(n, body, first=0):
        lax.fori_loop(first, n, lambda i, c: (body(i), c)[1], 0)

    def hold(a, q):
        def start(i):
            keep(a, q, piece(a, q, i), fulls[a][q].at[mp * own + i]).start()

        loop(own, start)

    def send_first(a):
        def start(i):
            to_y(a, 0, piece(a, 0, i), fulls[a][0].at[mp * own + i]).start()

        loop(own, start)

    def send_all(a, lead):
        if lead:
            send_first(a)
        for q in range(NQ):
            hold(a, q)
        for q in range(NQ):
            landed(keep, a, q, mp).wait()
            if q or not lead:
                landed(to_y, a, q, mp).start()
            landed(to_core, a, q, mp).start()

    for a in range(2):
        @pl.when(y != a)
        def _(a=a):
            send_all(a, True)
            send_all(1 - a, False)

    for cp in weights():
        cp.start()

    def z_rows(slot, q):
        return rows_at((q * nz + slot) * tc, tc)

    def z_main(b, slot, q):
        return remote(
            xg.at[y, pl.ds(b * GROUP, GROUP), pl.ds(q * tc, tc)],
            xall.at[y, :, z_rows(slot, q)],
            z_send.at[b, q], z_recv.at[q], ((2 * core + b) * 2 + x, mp),
        )

    def z_both(b, slot, q):
        return remote(
            xg.at[1 - y, pl.ds(b * GROUP, BOTHS[q]), pl.ds(q * tc, tc)],
            xall.at[1 - y, pl.ds(0, BOTHS[q]), z_rows(slot, q)],
            b_send.at[b, q], b_recv.at[q], ((2 * core + b) * 2 + x, mp),
        )

    def near_rows(q, first=1):
        return pl.ds((q * nz + first) * tc, (nz - first) * tc)

    def y_forward(a, q):
        part = xall.at[a, pl.ds(BOTHS[q], GROUP - BOTHS[q]), near_rows(q)]
        return remote(part, part, yf_send.at[q], yf_recv.at[q], other_y)

    def z_landed(a, q, n, sem):
        part = xall.at[a, pl.ds(0, n), near_rows(q)]
        return remote(part, part, yf_send.at[q], sem.at[q], other_y)

    def to_groups(send, q):
        for b in range(2):
            @pl.when(2 * core + b != z)
            def _(b=b):
                send(b, (z - 2 * core - b + nz) % nz, q).start()

    def pass_on(q):
        @pl.when(heavy)
        def _():
            z_landed(y, q, GROUP, z_recv).wait_recv()
            y_forward(y, q).start()

    def gather(a, q):
        landed(to_y, a, q, g_y).wait_recv()
        forward(a, q, g_y).start()
        landed(to_core, a, q, g_core).wait_recv()
        forward(a, q, g_far).wait_recv()

        def pack(i):
            xg[a, i, pl.ds(q * tc, tc)] = fulls[a][q][idx[a, i]]

        loop(hb, pack)

        @pl.when(heavy)
        def _():
            def own_rows(r):
                xall[a, r, z_rows(0, q)] = xg[a, hbase + r, pl.ds(q * tc, tc)]

            loop(GROUP, own_rows)

    def hidden_math(xs, dys, j):
        wi = wall[0, j].reshape(len(MASKS) * side, side)
        wo = jnp.concatenate([wall[1, j, k] for k in range(len(MASKS))], axis=1)
        pre = dot(jnp.concatenate(xs, axis=1), wi, ((1,), (0,)))
        d_act = dot(jnp.concatenate(dys, axis=1), wo, ((1,), (1,)))
        sq = pre * pre
        th = jnp.tanh(pre * (C0 + (C0 * C1) * sq))
        half = 0.5 + 0.5 * th
        value = pre * half
        slope = half + value * (1.0 - th) * (C0 + (3.0 * C0 * C1) * sq)
        return value.astype(jnp.bfloat16), (d_act * slope).astype(jnp.bfloat16)

    ht = tok // HALVES
    per = NQ // HALVES

    def hidden(h, first=0, last=hb):
        at = pl.ds(h * ht, ht)

        def one(j):
            act[j, at], dpre[j, at] = hidden_math(
                [xg[0, flip(j, m), at] for m in MASKS], [xg[1, flip(j, m), at] for m in MASKS], j
            )

        loop(last, one, first)

    def place(h, u):
        at = pl.ds(h * ht, ht)
        vs = [flip(u, m) for m in MASKS]
        wo = jnp.concatenate([wall[1, v, k] for k, v in enumerate(vs)], axis=0)
        wi = jnp.concatenate([wall[0, v, k] for k, v in enumerate(vs)], axis=1)
        out = dot(jnp.concatenate([act[v, at] for v in vs], axis=1), wo, ((1,), (0,)))
        back = dot(jnp.concatenate([dpre[v, at] for v in vs], axis=1), wi, ((1,), (1,)))
        for a, value in ((0, out), (1, back)):
            value = value.astype(jnp.bfloat16)
            for p in range(per):
                fulls[a][h * per + p][u] = value[p * tc : (p + 1) * tc]

    tables = (1, 0)

    def swap(a, q):
        return remote(
            fulls[a][q].at[pl.ds(hb, hb)], crecv.at[a, :, pl.ds(q * tc, tc)],
            o_send.at[a, q], o_recv.at[a, q], other_core,
        )

    def clear(h):
        for q in range(h * per, (h + 1) * per):
            for a in range(2):
                forward(a, q, g_y).wait_send()
                landed(to_y, a, q, mp).wait_send()
                landed(to_core, a, q, mp).wait_send()
                fulls[a][q][blocks] = jnp.zeros((tc, side), jnp.bfloat16)

    def hand_over(h):
        for a in range(2):
            for q in range(h * per, (h + 1) * per):
                for yy in range(2):
                    def fill(i, a=a, yy=yy, q=q):
                        fulls[a][q][hb + yy * own + i] = fulls[a][q][
                            idx[tables[a], hb + (2 * yy + 1 - core) * own + i]
                        ]
                    loop(own, fill)
                swap(a, q).start()

    def to_part(a, h, i):
        at = pl.ds(h * ht, ht)
        return remote(
            crecv.at[a, (1 - y) * own + i, at], xg.at[a, i, at], p_send, p_recv.at[h], other_y
        )

    def put(a, h, i):
        at = pl.ds(h * ht, ht)
        return pltpu.make_async_copy(crecv.at[a, y * own + i, at], outs[a].at[at, lanes(i)], out_sem)

    def finish(h):
        at = pl.ds(h * ht, ht)
        part = xg.at[:, pl.ds(0, own), at]
        remote(part, part, p_send, p_recv.at[h], other_y).wait_recv()
        for a in range(2):
            def one(i, a=a):
                crecv[a, y * own + i, at] = (
                    crecv[a, y * own + i, at].astype(jnp.float32) + xg[a, i, at].astype(jnp.float32)
                ).astype(jnp.bfloat16)
                put(a, h, i).start()

            loop(own, one)

    def merge(h):
        for a in range(2):
            for q in range(h * per, (h + 1) * per):
                swap(a, q).wait_recv()
                at = pl.ds(q * tc, tc)
                for yy in range(2):
                    def join(i, a=a, yy=yy, q=q, at=at):
                        crecv[a, yy * own + i, at] = crecv[a, yy * own + i, at] + fulls[a][q][
                            idx[tables[a], hb + (2 * yy + core) * own + i]
                        ]
                    loop(own, join)

    def emit(h):
        pl.semaphore_wait(free_sem.at[h], 1)
        for a in range(2):
            loop(own, lambda i, a=a: to_part(a, h, i).start())

    def near(q):
        y_forward(1 - y, q).wait_recv()
        if BOTHS[q]:
            z_landed(1 - y, q, BOTHS[q], b_recv).wait_recv()
        late = q >= per
        at = near_rows(q, 0 if late else 1)
        mine_at, own_at = pl.ds(q * tc, tc), z_rows(0, q)

        def one(r):
            acth[r, at], dpreh[r, at] = hidden_math(
                [xall[0, flip(r, m), at] for m in MASKS], [xall[1, flip(r, m), at] for m in MASKS], hbase + r
            )
            if late:
                act[hbase + r, mine_at], dpre[hbase + r, mine_at] = acth[r, own_at], dpreh[r, own_at]
            else:
                acth[r, own_at], dpreh[r, own_at] = act[hbase + r, mine_at], dpre[hbase + r, mine_at]

        loop(GROUP, one)

    for q in range(NQ):
        for a in range(2):
            @pl.when(y == a)
            def _(a=a, q=q):
                gather(a, q)

        to_groups(z_main, q)
    for cp in weights():
        cp.wait()
    for q in range(NQ):
        for a in range(2):
            @pl.when(y != a)
            def _(a=a, q=q):
                gather(a, q)

        if BOTHS[q]:
            to_groups(z_both, q)
        if q:
            pass_on(q - 1)
        if q == per - 1:
            hidden(0)
            clear(0)
            loop(hb, lambda u: place(0, u))
            hand_over(0)
    pass_on(NQ - 1)
    merge(0)
    clear(1)

    def release(h):
        for q in range(h * per, (h + 1) * per):
            for b in range(2):
                @pl.when(2 * core + b != z)
                def _(b=b, q=q):
                    z_main(b, 0, q).wait_send()
                    if BOTHS[q]:
                        z_both(b, 0, q).wait_send()

        pl.semaphore_signal(free_sem.at[h], inc=1, device_id=other_y, device_id_type=MESH)

    @pl.when(heavy)
    def _():
        for q in range(NQ - 1):
            near(q)
        release(0)
        near(NQ - 1)
        pl.semaphore_signal(go_sem, inc=1, device_id=other_core, device_id_type=MESH)
        emit(0)

    @pl.when(jnp.logical_not(heavy))
    def _():
        hidden(1)
        loop(hb, lambda u: place(1, u))
        hand_over(1)
        release(0)
        release(1)
        pl.semaphore_wait(go_sem, 1)
        emit(0)
        merge(1)
        emit(1)

    def to_x(r, a):
        return remote(
            theirs.at[r % SLOTS, a], arrived.at[r, a], g_send.at[r % SLOTS, a], g_recv.at[r, a], other_x
        )

    def to_z(r, a, zd, b):
        return remote(
            mine.at[r, a, :, zd], red.at[a, b * GROUP + r],
            r_send, r_recv.at[b], (zd * 2 + x, mp),
        )

    def keep_z(r, a):
        return pltpu.make_async_copy(mine.at[r, a, :, z], red.at[a, hbase + r], rl_sem)

    def settle(r, a):
        to_x(r, a).wait_recv()
        mine[r, a] = (
            mine[r, a].astype(jnp.float32) + arrived[r, a].astype(jnp.float32)
        ).astype(jnp.bfloat16)
        for dz in (2, 1, 3):
            to_z(r, a, (z + dz) % nz, z % 2).start()
        keep_z(r, a).start()

    @pl.when(heavy)
    def _():
        def grads(r, stage=2):
            for a in range(2):
                @pl.when(r >= SLOTS)
                def _(a=a):
                    to_x(r - SLOTS, a).wait_send()

                for k, m in enumerate(MASKS):
                    if a == 0:
                        value = dot(xall[0, flip(r, m)], dpreh[r], ((0,), (0,)))
                    else:
                        value = dot(acth[r], xall[1, flip(r, m)], ((0,), (0,)))
                    value = value.astype(jnp.bfloat16).reshape(nz, 2, rows, side)
                    low, high = value[:, 0], value[:, 1]
                    mine[r, a, k] = jnp.where(x == 0, low, high)
                    theirs[r % SLOTS, a, k] = jnp.where(x == 0, high, low)
                to_x(r, a).start()

                if stage == 0:
                    first = GROUP - hbase + a * (GROUP // 2)
                    hidden(1, first, first + GROUP // 2)
                if stage == 1:
                    step = 2 * (r - 1) + a
                    loop((step + 1) * (hb // 4), lambda u: place(1, u), step * (hb // 4))

                @pl.when(r > 0)
                def _(a=a):
                    settle(r - 1, a)

        grads(0, 0)
        loop(3, functools.partial(grads, stage=1), 1)
        hand_over(1)
        release(1)
        loop(4, grads, 3)
        merge(1)
        emit(1)
        loop(6, grads, 4)
        finish(0)
        loop(GROUP, grads, 6)
        settle(GROUP - 1, 0)
        settle(GROUP - 1, 1)

    @pl.when(jnp.logical_not(heavy))
    def _():
        finish(0)

    finish(1)
    for q in range(NQ):
        for a in range(2):
            swap(a, q).wait_send()

        @pl.when(heavy)
        def _(q=q):
            y_forward(y, q).wait_send()

    remote(crecv.at[0], crecv.at[0], p_send, p_recv.at[0], other_y).wait_send()
    pltpu.make_async_copy(crecv.at[0], crecv.at[0], out_sem).wait()

    @pl.when(heavy)
    def _():
        for r in range(GROUP - SLOTS, GROUP):
            for a in range(2):
                to_x(r, a).wait_send()
        group = red.at[:, pl.ds(hbase, GROUP)]
        pltpu.make_async_copy(group, group, rl_sem).wait()
        sent = mine.at[pl.ds(0, GROUP * (nz - 1) // nz)]
        remote(sent, sent, r_send, r_recv.at[0], other_x).wait_send()

    for b in range(2):
        @pl.when(2 * core + b != z)
        def _(b=b):
            got = red.at[:, pl.ds(b * GROUP, GROUP)]
            remote(got, got, r_send, r_recv.at[b], other_x).wait_recv()


def shards_fused(ndp, nmp, tokens, cotangent, w_in, w_out, in_blocks, out_blocks):
    hb, kk, side, _ = w_in.shape
    tok, feats = tokens.shape
    own = feats // side
    blocks = own * nmp
    nz = ndp // 2
    rows = side // ndp
    tc = tok // NQ
    first = jnp.stack([in_blocks[:, 0], out_blocks[:, 0]])
    place = jnp.arange(hb, dtype=jnp.int32)[:, None]
    hit = first[:, :, None] == jnp.arange(blocks, dtype=jnp.int32)
    table = jnp.concatenate([first, jnp.min(jnp.where(hit, place, blocks), axis=1)], axis=1)
    bf = jnp.bfloat16
    any_spec = pl.BlockSpec(memory_space=pl.ANY)
    smem = pl.BlockSpec(memory_space=pltpu.SMEM)
    dma = pltpu.SemaphoreType.DMA
    output, grad_tokens, red = pl.pallas_call(
        functools.partial(fused_kernel, (ndp, nmp, hb, side, own, tok, rows)),
        out_shape=(
            jax.ShapeDtypeStruct((tok, feats), bf),
            jax.ShapeDtypeStruct((tok, feats), bf),
            jax.ShapeDtypeStruct((2, hb, kk, rows, side), bf),
        ),
        in_specs=[smem] + [any_spec] * 4,
        out_specs=(any_spec,) * 3,
        scratch_shapes=[pltpu.VMEM((blocks + 1, tc, side), bf)] * (2 * NQ)
        + [
            pltpu.VMEM((2, hb, tok, side), bf),
            pltpu.VMEM((2, GROUP, nz * tok, side), bf),
            pltpu.VMEM((hb, tok, side), bf),
            pltpu.VMEM((hb, tok, side), bf),
            pltpu.VMEM((GROUP, nz * tok, side), bf),
            pltpu.VMEM((GROUP, nz * tok, side), bf),
            pltpu.VMEM((GROUP, 2, kk, nz, rows, side), bf),
            pltpu.VMEM((SLOTS, 2, kk, nz, rows, side), bf),
            pltpu.VMEM((GROUP, 2, kk, nz, rows, side), bf),
            pltpu.VMEM((2, hb, kk, side, side), bf),
            pltpu.VMEM((2, hb, tok, side), bf),
        ]
        + [dma((2, NQ))] * 9
        + [dma((NQ,))] * 4
        + [pltpu.SemaphoreType.REGULAR, dma((2,)), pltpu.SemaphoreType.REGULAR((2,))]
        + [dma((2, NQ))] * 2
        + [dma, dma((2,)), dma]
        + [dma((SLOTS, 2)), dma((GROUP, 2))]
        + [dma, dma((2,)), dma],
        compiler_params=pltpu.CompilerParams(
            collective_id=0, has_side_effects=True, vmem_limit_bytes=67_000_000
        ),
    )(
        table,
        tokens, cotangent, w_in, w_out,
    )
    scale = 1.0 / math.sqrt(tok * ndp)
    wide = jnp.float32

    return output, grad_tokens, red[0].astype(wide) * scale, red[1].astype(wide) * scale


def solution(mesh):
    ndp, nmp = mesh.shape["dp"], mesh.shape["mp"]

    def shards(tokens, cotangent, w_in, w_out, in_blocks, out_blocks):
        hb, kk, side, _ = w_in.shape
        blocks = tokens.shape[1] * nmp // side
        fits = (
            nmp == 4
            and kk == len(MASKS)
            and ndp == 2 * nmp
            and blocks == GROUP * nmp
            and 2 * hb == blocks
            and tokens.shape[0] % (16 * NQ) == 0
            and side % (16 * ndp) == 0
        )
        args = (tokens, cotangent, w_in, w_out, in_blocks, out_blocks)
        if fits:
            return shards_fused(ndp, nmp, *args)
        return shards_plain(*args)

    placed = (
        P("dp", "mp"),
        P("dp", "mp"),
        P("mp", None, None, None),
        P("mp", None, None, None),
        P("mp", None),
        P("mp", None),
    )
    return jax.shard_map(
        shards,
        mesh=mesh,
        in_specs=placed,
        out_specs=(
            P("dp", "mp"),
            P("dp", "mp"),
            P("mp", None, "dp", None),
            P("mp", None, "dp", None),
        ),
        check_vma=False,
    )
```

```python
import functools
import math

import jax
import jax.numpy as jnp
from jax import lax
from jax.experimental import pallas as pl
from jax.experimental.pallas import tpu as pltpu
from jax.sharding import PartitionSpec as P

MB = 2
MASKS = (0, 1, 2, 4)
MESH = pl.DeviceIdType.MESH
C0 = math.sqrt(2.0 / math.pi)
C1 = 0.044715
GROUP = 8
NQ = 4
BOTHS = (0, 0, 5, 5)
SLOTS = 4
PIECES = 4
HALVES = 2


def place_blocks(values, targets, row_blocks):
    step_tok = values.shape[0]
    side = values.shape[-1]
    flat = values.reshape(step_tok, -1, side)
    placed = (
        jnp.zeros((step_tok, row_blocks, side), jnp.float32).at[:, targets.reshape(-1)].add(flat)
    )
    return placed.reshape(step_tok, row_blocks * side)


def shards_plain(tokens, cotangent, w_in, w_out, in_blocks, out_blocks):
    hb_dev, kk, side, _ = w_in.shape
    total_tok = tokens.shape[0]
    width = tokens.shape[1] * lax.axis_size("mp")
    row_blocks = width // side
    passes = MB
    step_tok = total_tok // passes
    grad_in = jnp.zeros(w_in.shape, jnp.float32)
    grad_out = jnp.zeros(w_out.shape, jnp.float32)
    out_share = None
    outputs = []
    backs = []
    for index in range(passes):
        x_part = tokens[index * step_tok : (index + 1) * step_tok]
        dy_part = cotangent[index * step_tok : (index + 1) * step_tok]
        x_full = lax.all_gather(x_part, "mp", axis=1, tiled=True)
        selected = x_full.reshape(step_tok, row_blocks, side)[:, in_blocks]
        pre = jnp.einsum("tjkb,jkbc->tjc", selected, w_in, preferred_element_type=jnp.float32)
        act = jax.nn.gelu(pre).astype(jnp.bfloat16)
        terms = jnp.einsum("tjb,jkbc->tjkc", act, w_out, preferred_element_type=jnp.float32)
        partial_out = place_blocks(terms, out_blocks, row_blocks)
        outputs.append(
            lax.psum_scatter(
                partial_out.astype(jnp.bfloat16), "mp", scatter_dimension=1, tiled=True
            )
        )
        dy_full = lax.all_gather(dy_part, "mp", axis=1, tiled=True)
        picked = dy_full.reshape(step_tok, row_blocks, side)[:, out_blocks]
        d_act = jnp.einsum("tjkc,jkbc->tjb", picked, w_out, preferred_element_type=jnp.float32)
        _, pullback = jax.vjp(jax.nn.gelu, pre)
        d_pre = pullback(d_act)[0].astype(jnp.bfloat16)
        grad_out = grad_out + jnp.einsum(
            "tjb,tjkc->jkbc", act, picked, preferred_element_type=jnp.float32
        )
        grad_in = grad_in + jnp.einsum(
            "tjkb,tjc->jkbc", selected, d_pre, preferred_element_type=jnp.float32
        )
        back = jnp.einsum("tjc,jkbc->tjkb", d_pre, w_in, preferred_element_type=jnp.float32)
        partial_back = place_blocks(back, in_blocks, row_blocks)
        backs.append(
            lax.psum_scatter(
                partial_back.astype(jnp.bfloat16), "mp", scatter_dimension=1, tiled=True
            )
        )
    scale = 1.0 / math.sqrt(total_tok * lax.axis_size("dp"))
    in_share, out_share = (
        lax.psum_scatter(
            grad_in.astype(jnp.bfloat16), "dp", scatter_dimension=2, tiled=True
        ).astype(jnp.float32),
        lax.psum_scatter(
            grad_out.astype(jnp.bfloat16), "dp", scatter_dimension=2, tiled=True
        ).astype(jnp.float32),
    )
    output = jnp.concatenate(outputs, axis=0)
    grad_tokens = jnp.concatenate(backs, axis=0)
    return (output, grad_tokens, in_share * scale, out_share * scale)


def flip(u, m):
    if m == 0:
        return u
    return u + m * (1 - 2 * ((u // m) % 2))


def dot(a, b, dims):
    return lax.dot_general(a, b, (dims, ((), ())), preferred_element_type=jnp.float32)


def fused_kernel(dims, idx, x_hbm, dy_hbm, win_hbm, wout_hbm, out_hbm, back_hbm, red, *scratch):
    ndp, nmp, hb, side, own, tok, rows = dims
    fulls = [scratch[a * NQ : (a + 1) * NQ] for a in range(2)]
    (
        xg, xall, act, dpre, acth, dpreh, mine, theirs, arrived, wall, crecv,
        own_sem, y_send, y_recv, c_send, c_recv, f_send, f_recv, z_send, b_send, z_recv, b_recv,
        yf_send, yf_recv, go_sem, w_sem,
        free_sem, o_send, o_recv, p_send, p_recv, out_sem, g_send, g_recv, r_send, r_recv, rl_sem,
    ) = scratch[2 * NQ :]
    nz = ndp // 2
    tc = tok // NQ
    blocks = own * nmp
    dp = lax.axis_index("dp")
    mp = lax.axis_index("mp")
    z, x = dp // 2, dp % 2
    y, core = mp // 2, mp % 2
    other_core = (dp, y * 2 + 1 - core)
    other_y = (dp, (1 - y) * 2 + core)
    other_x = (z * 2 + 1 - x, mp)
    g_core = other_core[1]
    g_y = other_y[1]
    g_far = (1 - y) * 2 + 1 - core
    heavy = core == z // 2
    hbase = (z % 2) * GROUP
    srcs = (x_hbm, dy_hbm)
    outs = (out_hbm, back_hbm)

    barrier = pltpu.get_barrier_semaphore()
    peers = [other_core, other_y, other_x] + [((dp + 2 * dz) % ndp, mp) for dz in range(1, nz)]
    for peer in peers:
        pl.semaphore_signal(barrier, inc=1, device_id=peer, device_id_type=MESH)
    pl.semaphore_wait(barrier, len(peers))

    def remote(src, dst, ssem, rsem, peer):
        return pltpu.make_async_remote_copy(
            src_ref=src, dst_ref=dst, send_sem=ssem, recv_sem=rsem,
            device_id=peer, device_id_type=MESH,
        )

    def lanes(i):
        return pl.ds(pl.multiple_of(i * side, side), side)

    def rows_at(base, n):
        return pl.ds(pl.multiple_of(base, tc), n)

    def held(a, q, slot):
        return fulls[a][q].at[pl.ds(slot * own, own)]

    def piece(a, q, i):
        return srcs[a].at[pl.ds(q * tc, tc), lanes(i)]

    def to_y(a, q, src, dst):
        return remote(src, dst, y_send.at[a, q], y_recv.at[a, q], other_y)

    def to_core(a, q, src, dst):
        return remote(src, dst, c_send.at[a, q], c_recv.at[a, q], other_core)

    def keep(a, q, src, dst):
        return pltpu.make_async_copy(src, dst, own_sem.at[a, q])

    def landed(send, a, q, slot):
        return send(a, q, held(a, q, slot), held(a, q, slot))

    def forward(a, q, slot):
        return remote(held(a, q, g_y), held(a, q, slot), f_send.at[a, q], f_recv.at[a, q], other_core)

    def weights():
        return (
            pltpu.make_async_copy(win_hbm, wall.at[0], w_sem.at[0]),
            pltpu.make_async_copy(wout_hbm, wall.at[1], w_sem.at[1]),
        )

    def loop(n, body, first=0):
        lax.fori_loop(first, n, lambda i, c: (body(i), c)[1], 0)

    def hold(a, q):
        def start(i):
            keep(a, q, piece(a, q, i), fulls[a][q].at[mp * own + i]).start()

        loop(own, start)

    def send_first(a):
        def start(i):
            to_y(a, 0, piece(a, 0, i), fulls[a][0].at[mp * own + i]).start()

        loop(own, start)

    def send_all(a, lead):
        if lead:
            send_first(a)
        for q in range(NQ):
            hold(a, q)
        for q in range(NQ):
            landed(keep, a, q, mp).wait()
            if q or not lead:
                landed(to_y, a, q, mp).start()
            landed(to_core, a, q, mp).start()

    for a in range(2):
        @pl.when(y != a)
        def _(a=a):
            send_all(a, True)
            send_all(1 - a, False)

    for cp in weights():
        cp.start()

    def z_rows(slot, q):
        return rows_at((q * nz + slot) * tc, tc)

    def z_main(b, slot, q):
        return remote(
            xg.at[y, pl.ds(b * GROUP, GROUP), pl.ds(q * tc, tc)],
            xall.at[y, :, z_rows(slot, q)],
            z_send.at[b, q], z_recv.at[q], ((2 * core + b) * 2 + x, mp),
        )

    def z_both(b, slot, q):
        return remote(
            xg.at[1 - y, pl.ds(b * GROUP, BOTHS[q]), pl.ds(q * tc, tc)],
            xall.at[1 - y, pl.ds(0, BOTHS[q]), z_rows(slot, q)],
            b_send.at[b, q], b_recv.at[q], ((2 * core + b) * 2 + x, mp),
        )

    def near_rows(q, first=1):
        return pl.ds((q * nz + first) * tc, (nz - first) * tc)

    def y_forward(a, q):
        part = xall.at[a, pl.ds(BOTHS[q], GROUP - BOTHS[q]), near_rows(q)]
        return remote(part, part, yf_send.at[q], yf_recv.at[q], other_y)

    def z_landed(a, q, n, sem):
        part = xall.at[a, pl.ds(0, n), near_rows(q)]
        return remote(part, part, yf_send.at[q], sem.at[q], other_y)

    def to_groups(send, q):
        for b in range(2):
            @pl.when(2 * core + b != z)
            def _(b=b):
                send(b, (z - 2 * core - b + nz) % nz, q).start()

    def pass_on(q):
        @pl.when(heavy)
        def _():
            z_landed(y, q, GROUP, z_recv).wait_recv()
            y_forward(y, q).start()

    def gather(a, q):
        landed(to_y, a, q, g_y).wait_recv()
        forward(a, q, g_y).start()
        landed(to_core, a, q, g_core).wait_recv()
        forward(a, q, g_far).wait_recv()

        def pack(i):
            xg[a, i, pl.ds(q * tc, tc)] = fulls[a][q][idx[a, i]]

        loop(hb, pack)

        @pl.when(heavy)
        def _():
            def own_rows(r):
                xall[a, r, z_rows(0, q)] = xg[a, hbase + r, pl.ds(q * tc, tc)]

            loop(GROUP, own_rows)

    def hidden_math(xs, dys, j):
        wi = wall[0, j].reshape(len(MASKS) * side, side)
        wo = jnp.concatenate([wall[1, j, k] for k in range(len(MASKS))], axis=1)
        pre = dot(jnp.concatenate(xs, axis=1), wi, ((1,), (0,)))
        d_act = dot(jnp.concatenate(dys, axis=1), wo, ((1,), (1,)))
        sq = pre * pre
        th = jnp.tanh(pre * (C0 + (C0 * C1) * sq))
        half = 0.5 + 0.5 * th
        value = pre * half
        slope = half + value * (1.0 - th) * (C0 + (3.0 * C0 * C1) * sq)
        return value.astype(jnp.bfloat16), (d_act * slope).astype(jnp.bfloat16)

    ht = tok // HALVES
    per = NQ // HALVES

    def hidden(h, first=0, last=hb):
        at = pl.ds(h * ht, ht)

        def one(j):
            act[j, at], dpre[j, at] = hidden_math(
                [xg[0, flip(j, m), at] for m in MASKS], [xg[1, flip(j, m), at] for m in MASKS], j
            )

        loop(last, one, first)

    def place(h, u):
        at = pl.ds(h * ht, ht)
        vs = [flip(u, m) for m in MASKS]
        wo = jnp.concatenate([wall[1, v, k] for k, v in enumerate(vs)], axis=0)
        wi = jnp.concatenate([wall[0, v, k] for k, v in enumerate(vs)], axis=1)
        out = dot(jnp.concatenate([act[v, at] for v in vs], axis=1), wo, ((1,), (0,)))
        back = dot(jnp.concatenate([dpre[v, at] for v in vs], axis=1), wi, ((1,), (1,)))
        for a, value in ((0, out), (1, back)):
            value = value.astype(jnp.bfloat16)
            for p in range(per):
                fulls[a][h * per + p][u] = value[p * tc : (p + 1) * tc]

    tables = (1, 0)

    def swap(a, q):
        return remote(
            fulls[a][q].at[pl.ds(hb, hb)], crecv.at[a, :, pl.ds(q * tc, tc)],
            o_send.at[a, q], o_recv.at[a, q], other_core,
        )

    def clear(h):
        for q in range(h * per, (h + 1) * per):
            for a in range(2):
                forward(a, q, g_y).wait_send()
                landed(to_y, a, q, mp).wait_send()
                landed(to_core, a, q, mp).wait_send()
                fulls[a][q][blocks] = jnp.zeros((tc, side), jnp.bfloat16)

    def hand_over(h):
        for a in range(2):
            for q in range(h * per, (h + 1) * per):
                for yy in range(2):
                    def fill(i, a=a, yy=yy, q=q):
                        fulls[a][q][hb + yy * own + i] = fulls[a][q][
                            idx[tables[a], hb + (2 * yy + 1 - core) * own + i]
                        ]
                    loop(own, fill)
                swap(a, q).start()

    def to_part(a, h, i):
        at = pl.ds(h * ht, ht)
        return remote(
            crecv.at[a, (1 - y) * own + i, at], xg.at[a, i, at], p_send, p_recv.at[h], other_y
        )

    def put(a, h, i):
        at = pl.ds(h * ht, ht)
        return pltpu.make_async_copy(crecv.at[a, y * own + i, at], outs[a].at[at, lanes(i)], out_sem)

    def finish(h):
        at = pl.ds(h * ht, ht)
        part = xg.at[:, pl.ds(0, own), at]
        remote(part, part, p_send, p_recv.at[h], other_y).wait_recv()
        for a in range(2):
            def one(i, a=a):
                crecv[a, y * own + i, at] = (
                    crecv[a, y * own + i, at].astype(jnp.float32) + xg[a, i, at].astype(jnp.float32)
                ).astype(jnp.bfloat16)
                put(a, h, i).start()

            loop(own, one)

    def merge(h):
        for a in range(2):
            for q in range(h * per, (h + 1) * per):
                swap(a, q).wait_recv()
                at = pl.ds(q * tc, tc)
                for yy in range(2):
                    def join(i, a=a, yy=yy, q=q, at=at):
                        crecv[a, yy * own + i, at] = crecv[a, yy * own + i, at] + fulls[a][q][
                            idx[tables[a], hb + (2 * yy + core) * own + i]
                        ]
                    loop(own, join)

    def emit(h):
        pl.semaphore_wait(free_sem.at[h], 1)
        for a in range(2):
            loop(own, lambda i, a=a: to_part(a, h, i).start())

    def near_landed(q):
        y_forward(1 - y, q).wait_recv()
        if BOTHS[q]:
            z_landed(1 - y, q, BOTHS[q], b_recv).wait_recv()

    def near(q, r):
        late = q >= per
        at = near_rows(q, 0 if late else 1)
        mine_at, own_at = pl.ds(q * tc, tc), z_rows(0, q)
        acth[r, at], dpreh[r, at] = hidden_math(
            [xall[0, flip(r, m), at] for m in MASKS], [xall[1, flip(r, m), at] for m in MASKS], hbase + r
        )
        if late:
            act[hbase + r, mine_at], dpre[hbase + r, mine_at] = acth[r, own_at], dpreh[r, own_at]
        else:
            acth[r, own_at], dpreh[r, own_at] = act[hbase + r, mine_at], dpre[hbase + r, mine_at]

    for q in range(NQ):
        for a in range(2):
            @pl.when(y == a)
            def _(a=a, q=q):
                gather(a, q)

        to_groups(z_main, q)
    for cp in weights():
        cp.wait()
    for q in range(NQ):
        for a in range(2):
            @pl.when(y != a)
            def _(a=a, q=q):
                gather(a, q)

        if BOTHS[q]:
            to_groups(z_both, q)
        if q:
            pass_on(q - 1)
        if q == per - 1:
            hidden(0)
            clear(0)
            loop(hb, lambda u: place(0, u))
            hand_over(0)
    pass_on(NQ - 1)
    merge(0)
    clear(1)

    def release(h):
        for q in range(h * per, (h + 1) * per):
            for b in range(2):
                @pl.when(2 * core + b != z)
                def _(b=b, q=q):
                    z_main(b, 0, q).wait_send()
                    if BOTHS[q]:
                        z_both(b, 0, q).wait_send()

        pl.semaphore_signal(free_sem.at[h], inc=1, device_id=other_y, device_id_type=MESH)

    @pl.when(heavy)
    def _():
        release(0)
        emit(0)
        for q in range(NQ - 1):
            near_landed(q)
            loop(GROUP, functools.partial(near, q))
        near_landed(NQ - 1)
        pl.semaphore_signal(go_sem, inc=1, device_id=other_core, device_id_type=MESH)
        near(NQ - 1, 0)

    @pl.when(jnp.logical_not(heavy))
    def _():
        hidden(1)
        loop(hb, lambda u: place(1, u))
        hand_over(1)
        release(0)
        release(1)
        pl.semaphore_wait(go_sem, 1)
        emit(0)
        merge(1)
        emit(1)

    def to_x(r, a):
        return remote(
            theirs.at[r % SLOTS, a], arrived.at[r, a], g_send.at[r % SLOTS, a], g_recv.at[r, a], other_x
        )

    def to_z(r, a, zd, b):
        return remote(
            mine.at[r, a, :, zd], red.at[a, b * GROUP + r],
            r_send, r_recv.at[b], (zd * 2 + x, mp),
        )

    def keep_z(r, a):
        return pltpu.make_async_copy(mine.at[r, a, :, z], red.at[a, hbase + r], rl_sem)

    def settle(r, a):
        to_x(r, a).wait_recv()
        mine[r, a] = (
            mine[r, a].astype(jnp.float32) + arrived[r, a].astype(jnp.float32)
        ).astype(jnp.bfloat16)
        for dz in (2, 1, 3):
            to_z(r, a, (z + dz) % nz, z % 2).start()
        keep_z(r, a).start()

    @pl.when(heavy)
    def _():
        def grads(r, stage=3):
            for a in range(2):
                @pl.when(r >= SLOTS)
                def _(a=a):
                    to_x(r - SLOTS, a).wait_send()

                for k, m in enumerate(MASKS):
                    if a == 0:
                        value = dot(xall[0, flip(r, m)], dpreh[r], ((0,), (0,)))
                    else:
                        value = dot(acth[r], xall[1, flip(r, m)], ((0,), (0,)))
                    value = value.astype(jnp.bfloat16).reshape(nz, 2, rows, side)
                    low, high = value[:, 0], value[:, 1]
                    mine[r, a, k] = jnp.where(x == 0, low, high)
                    theirs[r % SLOTS, a, k] = jnp.where(x == 0, high, low)
                to_x(r, a).start()

                if stage == 0 and a == 1:
                    loop(GROUP, functools.partial(near, NQ - 1), 1)
                if stage == 1:
                    first = GROUP - hbase + a * (GROUP // 2)
                    hidden(1, first, first + GROUP // 2)
                if stage == 2:
                    step = 2 * (r - 2) + a
                    loop((step + 1) * (hb // 4), lambda u: place(1, u), step * (hb // 4))

                @pl.when(r > 0)
                def _(a=a):
                    settle(r - 1, a)

        grads(0, 0)
        grads(1, 1)
        loop(4, functools.partial(grads, stage=2), 2)
        hand_over(1)
        release(1)
        loop(5, grads, 4)
        merge(1)
        emit(1)
        loop(6, grads, 5)
        finish(0)
        loop(GROUP, grads, 6)
        settle(GROUP - 1, 0)
        settle(GROUP - 1, 1)

    @pl.when(jnp.logical_not(heavy))
    def _():
        finish(0)

    finish(1)
    for q in range(NQ):
        for a in range(2):
            swap(a, q).wait_send()

        @pl.when(heavy)
        def _(q=q):
            y_forward(y, q).wait_send()

    remote(crecv.at[0], crecv.at[0], p_send, p_recv.at[0], other_y).wait_send()
    pltpu.make_async_copy(crecv.at[0], crecv.at[0], out_sem).wait()

    @pl.when(heavy)
    def _():
        for r in range(GROUP - SLOTS, GROUP):
            for a in range(2):
                to_x(r, a).wait_send()
        group = red.at[:, pl.ds(hbase, GROUP)]
        pltpu.make_async_copy(group, group, rl_sem).wait()
        sent = mine.at[pl.ds(0, GROUP * (nz - 1) // nz)]
        remote(sent, sent, r_send, r_recv.at[0], other_x).wait_send()

    for b in range(2):
        @pl.when(2 * core + b != z)
        def _(b=b):
            got = red.at[:, pl.ds(b * GROUP, GROUP)]
            remote(got, got, r_send, r_recv.at[b], other_x).wait_recv()


def write_kernel(
    scale, out_hbm, back_hbm, red, out, back, grad_in, grad_out, kept, low, high, k_in, k_out, r_in, r_out
):
    n = red.shape[1] // PIECES
    srcs, dsts, grads = (out_hbm, back_hbm), (out, back), (grad_in, grad_out)

    def load(a, p):
        at = pl.ds(p * n, n)
        return pltpu.make_async_copy(red.at[a, at], low.at[a, at], r_in.at[a, p])

    def save(a, p):
        at = pl.ds(p * n, n)
        return pltpu.make_async_copy(high.at[a, at], grads[a].at[at], r_out.at[a, p])

    def take(a):
        return pltpu.make_async_copy(srcs[a], kept.at[a], k_in.at[a])

    def give(a):
        return pltpu.make_async_copy(kept.at[a], dsts[a], k_out.at[a])

    for p in range(PIECES):
        for a in range(2):
            load(a, p).start()
    for a in range(2):
        take(a).start()
    for p in range(PIECES):
        for a in range(2):
            load(a, p).wait()
            at = pl.ds(p * n, n)
            high[a, at] = low[a, at].astype(jnp.float32) * scale
            save(a, p).start()
    for a in range(2):
        take(a).wait()
        give(a).start()
    for a in range(2):
        for p in range(PIECES):
            save(a, p).wait()
        give(a).wait()


def shards_fused(ndp, nmp, tokens, cotangent, w_in, w_out, in_blocks, out_blocks):
    hb, kk, side, _ = w_in.shape
    tok, feats = tokens.shape
    own = feats // side
    blocks = own * nmp
    nz = ndp // 2
    rows = side // ndp
    tc = tok // NQ
    first = jnp.stack([in_blocks[:, 0], out_blocks[:, 0]])
    place = jnp.arange(hb, dtype=jnp.int32)[:, None]
    hit = first[:, :, None] == jnp.arange(blocks, dtype=jnp.int32)
    table = jnp.concatenate([first, jnp.min(jnp.where(hit, place, blocks), axis=1)], axis=1)
    bf = jnp.bfloat16
    any_spec = pl.BlockSpec(memory_space=pl.ANY)
    smem = pl.BlockSpec(memory_space=pltpu.SMEM)
    dma = pltpu.SemaphoreType.DMA
    output, grad_tokens, red = pl.pallas_call(
        functools.partial(fused_kernel, (ndp, nmp, hb, side, own, tok, rows)),
        out_shape=(
            jax.ShapeDtypeStruct((tok, feats), bf),
            jax.ShapeDtypeStruct((tok, feats), bf),
            jax.ShapeDtypeStruct((2, hb, kk, rows, side), bf),
        ),
        in_specs=[smem] + [any_spec] * 4,
        out_specs=(any_spec,) * 3,
        scratch_shapes=[pltpu.VMEM((blocks + 1, tc, side), bf)] * (2 * NQ)
        + [
            pltpu.VMEM((2, hb, tok, side), bf),
            pltpu.VMEM((2, GROUP, nz * tok, side), bf),
            pltpu.VMEM((hb, tok, side), bf),
            pltpu.VMEM((hb, tok, side), bf),
            pltpu.VMEM((GROUP, nz * tok, side), bf),
            pltpu.VMEM((GROUP, nz * tok, side), bf),
            pltpu.VMEM((GROUP, 2, kk, nz, rows, side), bf),
            pltpu.VMEM((SLOTS, 2, kk, nz, rows, side), bf),
            pltpu.VMEM((GROUP, 2, kk, nz, rows, side), bf),
            pltpu.VMEM((2, hb, kk, side, side), bf),
            pltpu.VMEM((2, hb, tok, side), bf),
        ]
        + [dma((2, NQ))] * 9
        + [dma((NQ,))] * 4
        + [pltpu.SemaphoreType.REGULAR, dma((2,)), pltpu.SemaphoreType.REGULAR((2,))]
        + [dma((2, NQ))] * 2
        + [dma, dma((2,)), dma]
        + [dma((SLOTS, 2)), dma((GROUP, 2))]
        + [dma, dma((2,)), dma],
        compiler_params=pltpu.CompilerParams(
            collective_id=0, has_side_effects=True, vmem_limit_bytes=67_000_000
        ),
    )(
        table,
        tokens, cotangent, w_in, w_out,
    )
    scale = 1.0 / math.sqrt(tok * ndp)
    wide = jnp.float32
    return pl.pallas_call(
        functools.partial(write_kernel, scale),
        out_shape=(
            jax.ShapeDtypeStruct((tok, feats), bf),
            jax.ShapeDtypeStruct((tok, feats), bf),
            jax.ShapeDtypeStruct((hb, kk, rows, side), wide),
            jax.ShapeDtypeStruct((hb, kk, rows, side), wide),
        ),
        in_specs=[any_spec] * 3,
        out_specs=(any_spec,) * 4,
        scratch_shapes=[
            pltpu.VMEM((2, tok, feats), bf),
            pltpu.VMEM((2, hb, kk, rows, side), bf),
            pltpu.VMEM((2, hb, kk, rows, side), wide),
            dma((2,)), dma((2,)), dma((2, PIECES)), dma((2, PIECES)),
        ],
        compiler_params=pltpu.CompilerParams(vmem_limit_bytes=67_000_000),
    )(output, grad_tokens, red)


def solution(mesh):
    ndp, nmp = mesh.shape["dp"], mesh.shape["mp"]

    def shards(tokens, cotangent, w_in, w_out, in_blocks, out_blocks):
        hb, kk, side, _ = w_in.shape
        blocks = tokens.shape[1] * nmp // side
        fits = (
            nmp == 4
            and kk == len(MASKS)
            and ndp == 2 * nmp
            and blocks == GROUP * nmp
            and 2 * hb == blocks
            and tokens.shape[0] % (16 * NQ) == 0
            and side % (16 * ndp) == 0
        )
        args = (tokens, cotangent, w_in, w_out, in_blocks, out_blocks)
        if fits:
            return shards_fused(ndp, nmp, *args)
        return shards_plain(*args)

    placed = (
        P("dp", "mp"),
        P("dp", "mp"),
        P("mp", None, None, None),
        P("mp", None, None, None),
        P("mp", None),
        P("mp", None),
    )
    return jax.shard_map(
        shards,
        mesh=mesh,
        in_specs=placed,
        out_specs=(
            P("dp", "mp"),
            P("dp", "mp"),
            P("mp", None, "dp", None),
            P("mp", None, "dp", None),
        ),
        check_vma=False,
    )
```

```python
import functools
import math

import jax
import jax.numpy as jnp
from jax import lax
from jax.experimental import pallas as pl
from jax.experimental.pallas import tpu as pltpu
from jax.sharding import PartitionSpec as P

MB = 2
MASKS = (0, 1, 2, 4)
MESH = pl.DeviceIdType.MESH
C0 = math.sqrt(2.0 / math.pi)
C1 = 0.044715
GROUP = 8
NQ = 4
LEAD = ((0, 3), (4, 1))
REST = ((3, 1), (5, 3))
RELAY = ((3, 1),)
BOTH = (5, 3)
SLOTS = 4
PIECES = 4
HALVES = 2


def place_blocks(values, targets, row_blocks):
    step_tok = values.shape[0]
    side = values.shape[-1]
    flat = values.reshape(step_tok, -1, side)
    placed = (
        jnp.zeros((step_tok, row_blocks, side), jnp.float32).at[:, targets.reshape(-1)].add(flat)
    )
    return placed.reshape(step_tok, row_blocks * side)


def shards_plain(tokens, cotangent, w_in, w_out, in_blocks, out_blocks):
    hb_dev, kk, side, _ = w_in.shape
    total_tok = tokens.shape[0]
    width = tokens.shape[1] * lax.axis_size("mp")
    row_blocks = width // side
    passes = MB
    step_tok = total_tok // passes
    grad_in = jnp.zeros(w_in.shape, jnp.float32)
    grad_out = jnp.zeros(w_out.shape, jnp.float32)
    out_share = None
    outputs = []
    backs = []
    for index in range(passes):
        x_part = tokens[index * step_tok : (index + 1) * step_tok]
        dy_part = cotangent[index * step_tok : (index + 1) * step_tok]
        x_full = lax.all_gather(x_part, "mp", axis=1, tiled=True)
        selected = x_full.reshape(step_tok, row_blocks, side)[:, in_blocks]
        pre = jnp.einsum("tjkb,jkbc->tjc", selected, w_in, preferred_element_type=jnp.float32)
        act = jax.nn.gelu(pre).astype(jnp.bfloat16)
        terms = jnp.einsum("tjb,jkbc->tjkc", act, w_out, preferred_element_type=jnp.float32)
        partial_out = place_blocks(terms, out_blocks, row_blocks)
        outputs.append(
            lax.psum_scatter(
                partial_out.astype(jnp.bfloat16), "mp", scatter_dimension=1, tiled=True
            )
        )
        dy_full = lax.all_gather(dy_part, "mp", axis=1, tiled=True)
        picked = dy_full.reshape(step_tok, row_blocks, side)[:, out_blocks]
        d_act = jnp.einsum("tjkc,jkbc->tjb", picked, w_out, preferred_element_type=jnp.float32)
        _, pullback = jax.vjp(jax.nn.gelu, pre)
        d_pre = pullback(d_act)[0].astype(jnp.bfloat16)
        grad_out = grad_out + jnp.einsum(
            "tjb,tjkc->jkbc", act, picked, preferred_element_type=jnp.float32
        )
        grad_in = grad_in + jnp.einsum(
            "tjkb,tjc->jkbc", selected, d_pre, preferred_element_type=jnp.float32
        )
        back = jnp.einsum("tjc,jkbc->tjkb", d_pre, w_in, preferred_element_type=jnp.float32)
        partial_back = place_blocks(back, in_blocks, row_blocks)
        backs.append(
            lax.psum_scatter(
                partial_back.astype(jnp.bfloat16), "mp", scatter_dimension=1, tiled=True
            )
        )
    scale = 1.0 / math.sqrt(total_tok * lax.axis_size("dp"))
    in_share, out_share = (
        lax.psum_scatter(
            grad_in.astype(jnp.bfloat16), "dp", scatter_dimension=2, tiled=True
        ).astype(jnp.float32),
        lax.psum_scatter(
            grad_out.astype(jnp.bfloat16), "dp", scatter_dimension=2, tiled=True
        ).astype(jnp.float32),
    )
    output = jnp.concatenate(outputs, axis=0)
    grad_tokens = jnp.concatenate(backs, axis=0)
    return (output, grad_tokens, in_share * scale, out_share * scale)


def flip(u, m):
    if m == 0:
        return u
    return u + m * (1 - 2 * ((u // m) % 2))


def dot(a, b, dims):
    return lax.dot_general(a, b, (dims, ((), ())), preferred_element_type=jnp.float32)


def fused_kernel(dims, idx, x_hbm, dy_hbm, win_hbm, wout_hbm, out_hbm, back_hbm, red, *scratch):
    ndp, nmp, hb, side, own, tok, rows = dims
    fulls = [scratch[a * NQ : (a + 1) * NQ] for a in range(2)]
    (
        xg, xall, act, dpre, acth, dpreh, mine, theirs, arrived, wall, crecv,
        own_sem, y_send, y_recv, c_send, c_recv, f_send, f_recv, za_send, zb_send, b_send,
        za_recv, zb_recv, b_recv, fa_send, fa_recv, fb_send, fb_recv, go_sem, w_sem,
        free_sem, o_send, o_recv, p_send, p_recv, out_sem, g_send, g_recv, x_send, x_recv, r_send, r_recv, rl_sem,
    ) = scratch[2 * NQ :]
    nz = ndp // 2
    tc = tok // NQ
    blocks = own * nmp
    dp = lax.axis_index("dp")
    mp = lax.axis_index("mp")
    z, x = dp // 2, dp % 2
    y, core = mp // 2, mp % 2
    other_core = (dp, y * 2 + 1 - core)
    other_y = (dp, (1 - y) * 2 + core)
    other_x = (z * 2 + 1 - x, mp)
    g_core = other_core[1]
    g_y = other_y[1]
    g_far = (1 - y) * 2 + 1 - core
    heavy = core == z // 2
    hbase = (z % 2) * GROUP
    srcs = (x_hbm, dy_hbm)
    outs = (out_hbm, back_hbm)

    barrier = pltpu.get_barrier_semaphore()
    peers = [other_core, other_y, other_x] + [((dp + 2 * dz) % ndp, mp) for dz in range(1, nz)]
    for peer in peers:
        pl.semaphore_signal(barrier, inc=1, device_id=peer, device_id_type=MESH)
    pl.semaphore_wait(barrier, len(peers))

    def remote(src, dst, ssem, rsem, peer):
        return pltpu.make_async_remote_copy(
            src_ref=src, dst_ref=dst, send_sem=ssem, recv_sem=rsem,
            device_id=peer, device_id_type=MESH,
        )

    def lanes(i):
        return pl.ds(pl.multiple_of(i * side, side), side)

    def rows_at(base, n):
        return pl.ds(pl.multiple_of(base, tc), n)

    def held(a, q, slot):
        return fulls[a][q].at[pl.ds(slot * own, own)]

    def piece(a, q, i):
        return srcs[a].at[pl.ds(q * tc, tc), lanes(i)]

    def to_y(a, q, src, dst):
        return remote(src, dst, y_send.at[a, q], y_recv.at[a, q], other_y)

    def to_core(a, q, src, dst):
        return remote(src, dst, c_send.at[a, q], c_recv.at[a, q], other_core)

    def keep(a, q, src, dst):
        return pltpu.make_async_copy(src, dst, own_sem.at[a, q])

    def landed(send, a, q, slot):
        return send(a, q, held(a, q, slot), held(a, q, slot))

    def forward(a, q, slot):
        return remote(held(a, q, g_y), held(a, q, slot), f_send.at[a, q], f_recv.at[a, q], other_core)

    def weights():
        return (
            pltpu.make_async_copy(win_hbm, wall.at[0], w_sem.at[0]),
            pltpu.make_async_copy(wout_hbm, wall.at[1], w_sem.at[1]),
        )

    def loop(n, body, first=0):
        lax.fori_loop(first, n, lambda i, c: (body(i), c)[1], 0)

    def hold(a, q):
        def start(i):
            keep(a, q, piece(a, q, i), fulls[a][q].at[mp * own + i]).start()

        loop(own, start)

    def send_first(a):
        def start(i):
            to_y(a, 0, piece(a, 0, i), fulls[a][0].at[mp * own + i]).start()

        loop(own, start)

    def send_all(a, lead):
        if lead:
            send_first(a)
        for q in range(NQ):
            hold(a, q)
        for q in range(NQ):
            landed(keep, a, q, mp).wait()
            if q or not lead:
                landed(to_y, a, q, mp).start()
            landed(to_core, a, q, mp).start()

    for a in range(2):
        @pl.when(y != a)
        def _(a=a):
            send_all(a, True)
            send_all(1 - a, False)

    for cp in weights():
        cp.start()

    def z_rows(slot, q):
        return rows_at((q * nz + slot) * tc, tc)

    def size(spans):
        return sum(n for _, n in spans)

    def z_span(a, b, slot, q, at, n, ssem, rsem):
        return remote(
            xg.at[a, pl.ds(b * GROUP + at, n), pl.ds(q * tc, tc)],
            xall.at[a, pl.ds(at, n), z_rows(slot, q)],
            ssem.at[b, q], rsem.at[q], ((2 * core + b) * 2 + x, mp),
        )

    def near_rows(q, first=1):
        return pl.ds((q * nz + first) * tc, (nz - first) * tc)

    def to_groups(a, q, spans, ssem, rsem):
        for b in range(2):
            @pl.when(2 * core + b != z)
            def _(b=b):
                for at, n in spans:
                    z_span(a, b, (z - 2 * core - b + nz) % nz, q, at, n, ssem, rsem).start()

    def z_sent(a, b, q, n, ssem, rsem):
        z_span(a, b, 0, q, 0, n, ssem, rsem).wait_send()

    def near_part(a, q, at, n, ssem, rsem):
        part = xall.at[a, pl.ds(at, n), near_rows(q)]
        return remote(part, part, ssem.at[q], rsem.at[q], other_y)

    def pass_on(q, spans, here, ssem, rsem, held_spans):
        @pl.when(heavy)
        def _():
            near_part(y, q, 0, size(held_spans), ssem, here).wait_recv()
            for at, n in spans:
                near_part(y, q, at, n, ssem, rsem).start()

    def pass_lead(q):
        pass_on(q, LEAD, za_recv, fa_send, fa_recv, LEAD)

    def pass_rest(q):
        pass_on(q, RELAY, zb_recv, fb_send, fb_recv, REST)

    def gather(a, q):
        landed(to_y, a, q, g_y).wait_recv()
        forward(a, q, g_y).start()
        landed(to_core, a, q, g_core).wait_recv()
        forward(a, q, g_far).wait_recv()

        def pack(i):
            xg[a, i, pl.ds(q * tc, tc)] = fulls[a][q][idx[a, i]]

        loop(hb, pack)

        @pl.when(heavy)
        def _():
            def own_rows(r):
                xall[a, r, z_rows(0, q)] = xg[a, hbase + r, pl.ds(q * tc, tc)]

            loop(GROUP, own_rows)

    def hidden_math(xs, dys, j):
        wi = wall[0, j].reshape(len(MASKS) * side, side)
        wo = jnp.concatenate([wall[1, j, k] for k in range(len(MASKS))], axis=1)
        pre = dot(jnp.concatenate(xs, axis=1), wi, ((1,), (0,)))
        d_act = dot(jnp.concatenate(dys, axis=1), wo, ((1,), (1,)))
        sq = pre * pre
        th = jnp.tanh(pre * (C0 + (C0 * C1) * sq))
        half = 0.5 + 0.5 * th
        value = pre * half
        slope = half + value * (1.0 - th) * (C0 + (3.0 * C0 * C1) * sq)
        return value.astype(jnp.bfloat16), (d_act * slope).astype(jnp.bfloat16)

    ht = tok // HALVES
    per = NQ // HALVES

    def hidden(h, first=0, last=hb):
        at = pl.ds(h * ht, ht)

        def one(j):
            act[j, at], dpre[j, at] = hidden_math(
                [xg[0, flip(j, m), at] for m in MASKS], [xg[1, flip(j, m), at] for m in MASKS], j
            )

        loop(last, one, first)

    def place(h, u):
        at = pl.ds(h * ht, ht)
        vs = [flip(u, m) for m in MASKS]
        wo = jnp.concatenate([wall[1, v, k] for k, v in enumerate(vs)], axis=0)
        wi = jnp.concatenate([wall[0, v, k] for k, v in enumerate(vs)], axis=1)
        out = dot(jnp.concatenate([act[v, at] for v in vs], axis=1), wo, ((1,), (0,)))
        back = dot(jnp.concatenate([dpre[v, at] for v in vs], axis=1), wi, ((1,), (1,)))
        for a, value in ((0, out), (1, back)):
            value = value.astype(jnp.bfloat16)
            for p in range(per):
                fulls[a][h * per + p][u] = value[p * tc : (p + 1) * tc]

    tables = (1, 0)

    def swap(a, q):
        return remote(
            fulls[a][q].at[pl.ds(hb, hb)], crecv.at[a, :, pl.ds(q * tc, tc)],
            o_send.at[a, q], o_recv.at[a, q], other_core,
        )

    def clear(h):
        for q in range(h * per, (h + 1) * per):
            for a in range(2):
                forward(a, q, g_y).wait_send()
                landed(to_y, a, q, mp).wait_send()
                landed(to_core, a, q, mp).wait_send()
                fulls[a][q][blocks] = jnp.zeros((tc, side), jnp.bfloat16)

    def hand_over(h):
        for a in range(2):
            for q in range(h * per, (h + 1) * per):
                for yy in range(2):
                    def fill(i, a=a, yy=yy, q=q):
                        fulls[a][q][hb + yy * own + i] = fulls[a][q][
                            idx[tables[a], hb + (2 * yy + 1 - core) * own + i]
                        ]
                    loop(own, fill)
                swap(a, q).start()

    def to_part(a, h, i):
        at = pl.ds(h * ht, ht)
        return remote(
            crecv.at[a, (1 - y) * own + i, at], xg.at[a, i, at], p_send, p_recv.at[h], other_y
        )

    def put(a, h, i):
        at = pl.ds(h * ht, ht)
        return pltpu.make_async_copy(crecv.at[a, y * own + i, at], outs[a].at[at, lanes(i)], out_sem)

    def finish(h):
        at = pl.ds(h * ht, ht)
        part = xg.at[:, pl.ds(0, own), at]
        remote(part, part, p_send, p_recv.at[h], other_y).wait_recv()
        for a in range(2):
            def one(i, a=a):
                crecv[a, y * own + i, at] = (
                    crecv[a, y * own + i, at].astype(jnp.float32) + xg[a, i, at].astype(jnp.float32)
                ).astype(jnp.bfloat16)
                put(a, h, i).start()

            loop(own, one)

    def merge(h):
        for a in range(2):
            for q in range(h * per, (h + 1) * per):
                swap(a, q).wait_recv()
                at = pl.ds(q * tc, tc)
                for yy in range(2):
                    def join(i, a=a, yy=yy, q=q, at=at):
                        crecv[a, yy * own + i, at] = crecv[a, yy * own + i, at] + fulls[a][q][
                            idx[tables[a], hb + (2 * yy + core) * own + i]
                        ]
                    loop(own, join)

    def emit(h):
        pl.semaphore_wait(free_sem.at[h], 1)
        for a in range(2):
            loop(own, lambda i, a=a: to_part(a, h, i).start())

    def near(r, p):
        at = pl.ds(pl.multiple_of(p * per * nz * tc, per * nz * tc), per * nz * tc)
        acth[r, at], dpreh[r, at] = hidden_math(
            [xall[0, flip(r, m), at] for m in MASKS], [xall[1, flip(r, m), at] for m in MASKS], hbase + r
        )

    def release(h):
        for q in range(h * per, (h + 1) * per):
            for b in range(2):
                @pl.when(2 * core + b != z)
                def _(b=b, q=q):
                    z_sent(y, b, q, size(LEAD), za_send, za_recv)
                    z_sent(y, b, q, size(REST), zb_send, zb_recv)
                    z_sent(1 - y, b, q, BOTH[1], b_send, b_recv)

        pl.semaphore_signal(free_sem.at[h], inc=1, device_id=other_y, device_id_type=MESH)

    for q in range(NQ):
        for a in range(2):
            @pl.when(y == a)
            def _(a=a, q=q):
                gather(a, q)

        to_groups(y, q, LEAD, za_send, za_recv)
    for q in range(NQ):
        to_groups(y, q, REST, zb_send, zb_recv)
    for cp in weights():
        cp.wait()
    for q in range(NQ):
        for a in range(2):
            @pl.when(y != a)
            def _(a=a, q=q):
                gather(a, q)

        to_groups(1 - y, q, (BOTH,), b_send, b_recv)
        if q == per - 1:
            hidden(0)
        if q == per:
            pass_lead(0)
            pass_lead(1)
            clear(0)
            loop(hb, lambda u: place(0, u))
    for q in range(per, NQ):
        pass_lead(q)
    hand_over(0)
    hidden(1)
    clear(1)
    merge(0)
    loop(hb // 2, lambda u: place(1, u))
    for q in range(NQ):
        pass_rest(q)
    nk = len(MASKS)

    def to_x(r, a, k=0, n=nk):
        ssem, rsem = (x_send, x_recv) if k else (g_send.at[r % SLOTS, a], g_recv.at[r, a])
        at = pl.ds(k, n)
        return remote(theirs.at[r % SLOTS, a, at], arrived.at[r, a, at], ssem, rsem, other_x)

    def to_z(r, a, zd, b, at):
        return remote(
            mine.at[r, a, at, zd], red.at[a, b * GROUP + r, at], r_send, r_recv.at[b], (zd * 2 + x, mp)
        )

    def settle(r, a, k=0, n=nk):
        to_x(r, a, k, n).wait_recv()
        at = pl.ds(k, n)
        mine[r, a, at] = (
            mine[r, a, at].astype(jnp.float32) + arrived[r, a, at].astype(jnp.float32)
        ).astype(jnp.bfloat16)
        for dz in (2, 1, 3):
            to_z(r, a, (z + dz) % nz, z % 2, at).start()
        pltpu.make_async_copy(mine.at[r, a, at, z], red.at[a, hbase + r, at], rl_sem).start()

    def step(r, a, first=0, n=nk):
        for k in range(first, first + n):
            block = flip(r, MASKS[k])
            if a == 0:
                value = dot(xall[0, block], dpreh[r], ((0,), (0,)))
            else:
                value = dot(acth[r], xall[1, block], ((0,), (0,)))
            value = value.astype(jnp.bfloat16).reshape(nz, 2, rows, side)
            low, high = value[:, 0], value[:, 1]
            mine[r, a, k] = jnp.where(x == 0, low, high)
            theirs[r % SLOTS, a, k] = jnp.where(x == 0, high, low)
        to_x(r, a, first, n).start()

    @pl.when(heavy)
    def _():
        def grads(r):
            for a in range(2):
                @pl.when(r >= SLOTS)
                def _(a=a):
                    to_x(r - SLOTS, a).wait_send()

                step(r, a)

                @pl.when(r > 0)
                def _(a=a):
                    settle(r - 1, a)

        def both_steps(r):
            loop(HALVES, functools.partial(near, r))
            grads(r)

        def landed_in(h, n, ssem, rsem):
            for q in range(h * per, (h + 1) * per):
                near_part(1 - y, q, 0, n, ssem, rsem).wait_recv()

        for h in range(HALVES):
            landed_in(h, size(LEAD), fa_send, fa_recv)
            near(0, h)
        grads(0)
        release(0)
        pl.semaphore_signal(go_sem, inc=1, device_id=other_core, device_id_type=MESH)
        emit(0)
        loop(hb, lambda u: place(1, u), hb // 2)
        for h in range(HALVES):
            landed_in(h, size(RELAY), fb_send, fb_recv)
            landed_in(h, BOTH[1], fb_send, b_recv)
            near(1, h)
        grads(1)
        hand_over(1)
        merge(1)
        release(1)
        emit(1)
        loop(6, both_steps, 2)
        finish(0)
        loop(GROUP - 1, both_steps, 6)
        last = GROUP - 1
        loop(HALVES, functools.partial(near, last))
        to_x(last - SLOTS, 0).wait_send()
        to_x(last - SLOTS, 1).wait_send()
        step(last, 0)
        settle(last - 1, 0)
        step(last, 1, 0, 2)
        settle(last - 1, 1)
        step(last, 1, 2, 2)
        settle(last, 0)
        settle(last, 1, 0, 2)
        settle(last, 1, 2, 2)

    @pl.when(jnp.logical_not(heavy))
    def _():
        loop(hb, lambda u: place(1, u), hb // 2)
        hand_over(1)
        release(0)
        release(1)
        pl.semaphore_wait(go_sem, 1)
        emit(0)
        merge(1)
        emit(1)
        finish(0)

    finish(1)

    for q in range(NQ):
        for a in range(2):
            swap(a, q).wait_send()

        @pl.when(heavy)
        def _(q=q):
            near_part(y, q, 0, size(LEAD), fa_send, fa_recv).wait_send()
            near_part(y, q, 0, size(RELAY), fb_send, fb_recv).wait_send()

    remote(crecv.at[0], crecv.at[0], p_send, p_recv.at[0], other_y).wait_send()
    pltpu.make_async_copy(crecv.at[0], crecv.at[0], out_sem).wait()

    @pl.when(heavy)
    def _():
        for r in range(GROUP - SLOTS, GROUP):
            for a in range(2):
                if a == 0 or r < GROUP - 1:
                    to_x(r, a).wait_send()
        to_x(GROUP - 1, 1, 0, 2).wait_send()
        to_x(GROUP - 1, 1, 2, 2).wait_send()
        group = red.at[:, pl.ds(hbase, GROUP)]
        pltpu.make_async_copy(group, group, rl_sem).wait()
        sent = mine.at[pl.ds(0, GROUP * (nz - 1) // nz)]
        remote(sent, sent, r_send, r_recv.at[0], other_x).wait_send()

    for b in range(2):
        @pl.when(2 * core + b != z)
        def _(b=b):
            got = red.at[:, pl.ds(b * GROUP, GROUP)]
            remote(got, got, r_send, r_recv.at[b], other_x).wait_recv()


def write_kernel(
    scale, out_hbm, back_hbm, red, out, back, grad_in, grad_out, kept, low, high, k_in, k_out, r_in, r_out
):
    n = red.shape[1] // PIECES
    srcs, dsts, grads = (out_hbm, back_hbm), (out, back), (grad_in, grad_out)

    def load(a, p):
        at = pl.ds(p * n, n)
        return pltpu.make_async_copy(red.at[a, at], low.at[a, at], r_in.at[a, p])

    def save(a, p):
        at = pl.ds(p * n, n)
        return pltpu.make_async_copy(high.at[a, at], grads[a].at[at], r_out.at[a, p])

    def take(a):
        return pltpu.make_async_copy(srcs[a], kept.at[a], k_in.at[a])

    def give(a):
        return pltpu.make_async_copy(kept.at[a], dsts[a], k_out.at[a])

    for p in range(PIECES):
        for a in range(2):
            load(a, p).start()
    for a in range(2):
        take(a).start()
    for p in range(PIECES):
        for a in range(2):
            load(a, p).wait()
            at = pl.ds(p * n, n)
            high[a, at] = low[a, at].astype(jnp.float32) * scale
            save(a, p).start()
    for a in range(2):
        take(a).wait()
        give(a).start()
    for a in range(2):
        for p in range(PIECES):
            save(a, p).wait()
        give(a).wait()


def shards_fused(ndp, nmp, tokens, cotangent, w_in, w_out, in_blocks, out_blocks):
    hb, kk, side, _ = w_in.shape
    tok, feats = tokens.shape
    own = feats // side
    blocks = own * nmp
    nz = ndp // 2
    rows = side // ndp
    tc = tok // NQ
    first = jnp.stack([in_blocks[:, 0], out_blocks[:, 0]])
    place = jnp.arange(hb, dtype=jnp.int32)[:, None]
    hit = first[:, :, None] == jnp.arange(blocks, dtype=jnp.int32)
    table = jnp.concatenate([first, jnp.min(jnp.where(hit, place, blocks), axis=1)], axis=1)
    bf = jnp.bfloat16
    any_spec = pl.BlockSpec(memory_space=pl.ANY)
    smem = pl.BlockSpec(memory_space=pltpu.SMEM)
    dma = pltpu.SemaphoreType.DMA
    output, grad_tokens, red = pl.pallas_call(
        functools.partial(fused_kernel, (ndp, nmp, hb, side, own, tok, rows)),
        out_shape=(
            jax.ShapeDtypeStruct((tok, feats), bf),
            jax.ShapeDtypeStruct((tok, feats), bf),
            jax.ShapeDtypeStruct((2, hb, kk, rows, side), bf),
        ),
        in_specs=[smem] + [any_spec] * 4,
        out_specs=(any_spec,) * 3,
        scratch_shapes=[pltpu.VMEM((blocks + 1, tc, side), bf)] * (2 * NQ)
        + [
            pltpu.VMEM((2, hb, tok, side), bf),
            pltpu.VMEM((2, GROUP, nz * tok, side), bf),
            pltpu.VMEM((hb, tok, side), bf),
            pltpu.VMEM((hb, tok, side), bf),
            pltpu.VMEM((GROUP, nz * tok, side), bf),
            pltpu.VMEM((GROUP, nz * tok, side), bf),
            pltpu.VMEM((GROUP, 2, kk, nz, rows, side), bf),
            pltpu.VMEM((SLOTS, 2, kk, nz, rows, side), bf),
            pltpu.VMEM((GROUP, 2, kk, nz, rows, side), bf),
            pltpu.VMEM((2, hb, kk, side, side), bf),
            pltpu.VMEM((2, hb, tok, side), bf),
        ]
        + [dma((2, NQ))] * 10
        + [dma((NQ,))] * 7
        + [pltpu.SemaphoreType.REGULAR, dma((2,)), pltpu.SemaphoreType.REGULAR((2,))]
        + [dma((2, NQ))] * 2
        + [dma, dma((2,)), dma]
        + [dma((SLOTS, 2)), dma((GROUP, 2))]
        + [dma, dma, dma, dma((2,)), dma],
        compiler_params=pltpu.CompilerParams(
            collective_id=0, has_side_effects=True, vmem_limit_bytes=67_000_000
        ),
    )(
        table,
        tokens, cotangent, w_in, w_out,
    )
    scale = 1.0 / math.sqrt(tok * ndp)
    wide = jnp.float32
    return pl.pallas_call(
        functools.partial(write_kernel, scale),
        out_shape=(
            jax.ShapeDtypeStruct((tok, feats), bf),
            jax.ShapeDtypeStruct((tok, feats), bf),
            jax.ShapeDtypeStruct((hb, kk, rows, side), wide),
            jax.ShapeDtypeStruct((hb, kk, rows, side), wide),
        ),
        in_specs=[any_spec] * 3,
        out_specs=(any_spec,) * 4,
        scratch_shapes=[
            pltpu.VMEM((2, tok, feats), bf),
            pltpu.VMEM((2, hb, kk, rows, side), bf),
            pltpu.VMEM((2, hb, kk, rows, side), wide),
            dma((2,)), dma((2,)), dma((2, PIECES)), dma((2, PIECES)),
        ],
        compiler_params=pltpu.CompilerParams(vmem_limit_bytes=67_000_000),
    )(output, grad_tokens, red)


def solution(mesh):
    ndp, nmp = mesh.shape["dp"], mesh.shape["mp"]

    def shards(tokens, cotangent, w_in, w_out, in_blocks, out_blocks):
        hb, kk, side, _ = w_in.shape
        blocks = tokens.shape[1] * nmp // side
        fits = (
            nmp == 4
            and kk == len(MASKS)
            and ndp == 2 * nmp
            and blocks == GROUP * nmp
            and 2 * hb == blocks
            and tokens.shape[0] % (16 * NQ) == 0
            and side % (16 * ndp) == 0
        )
        args = (tokens, cotangent, w_in, w_out, in_blocks, out_blocks)
        if fits:
            return shards_fused(ndp, nmp, *args)
        return shards_plain(*args)

    placed = (
        P("dp", "mp"),
        P("dp", "mp"),
        P("mp", None, None, None),
        P("mp", None, None, None),
        P("mp", None),
        P("mp", None),
    )
    return jax.shard_map(
        shards,
        mesh=mesh,
        in_specs=placed,
        out_specs=(
            P("dp", "mp"),
            P("dp", "mp"),
            P("mp", None, "dp", None),
            P("mp", None, "dp", None),
        ),
        check_vma=False,
    )
```

```python
import functools
import math

import jax
import jax.numpy as jnp
from jax import lax
from jax.experimental import pallas as pl
from jax.experimental.pallas import tpu as pltpu
from jax.sharding import PartitionSpec as P

MB = 2
MASKS = (0, 1, 2, 4)
MESH = pl.DeviceIdType.MESH
C0 = math.sqrt(2.0 / math.pi)
C1 = 0.044715
GROUP = 8
NQ = 4
LEAD = ((0, 3), (4, 1))
REST = ((3, 1), (5, 3))
RELAYS = (((3, 1),), ((3, 1),), ((3, 1), (5, 1)), ((3, 1), (5, 1)))
BOTHS = ((5, 3), (5, 3), (6, 2), (6, 2))
SLOTS = 4
PIECES = 4
HALVES = 2


def place_blocks(values, targets, row_blocks):
    step_tok = values.shape[0]
    side = values.shape[-1]
    flat = values.reshape(step_tok, -1, side)
    placed = (
        jnp.zeros((step_tok, row_blocks, side), jnp.float32).at[:, targets.reshape(-1)].add(flat)
    )
    return placed.reshape(step_tok, row_blocks * side)


def shards_plain(tokens, cotangent, w_in, w_out, in_blocks, out_blocks):
    hb_dev, kk, side, _ = w_in.shape
    total_tok = tokens.shape[0]
    width = tokens.shape[1] * lax.axis_size("mp")
    row_blocks = width // side
    passes = MB
    step_tok = total_tok // passes
    grad_in = jnp.zeros(w_in.shape, jnp.float32)
    grad_out = jnp.zeros(w_out.shape, jnp.float32)
    out_share = None
    outputs = []
    backs = []
    for index in range(passes):
        x_part = tokens[index * step_tok : (index + 1) * step_tok]
        dy_part = cotangent[index * step_tok : (index + 1) * step_tok]
        x_full = lax.all_gather(x_part, "mp", axis=1, tiled=True)
        selected = x_full.reshape(step_tok, row_blocks, side)[:, in_blocks]
        pre = jnp.einsum("tjkb,jkbc->tjc", selected, w_in, preferred_element_type=jnp.float32)
        act = jax.nn.gelu(pre).astype(jnp.bfloat16)
        terms = jnp.einsum("tjb,jkbc->tjkc", act, w_out, preferred_element_type=jnp.float32)
        partial_out = place_blocks(terms, out_blocks, row_blocks)
        outputs.append(
            lax.psum_scatter(
                partial_out.astype(jnp.bfloat16), "mp", scatter_dimension=1, tiled=True
            )
        )
        dy_full = lax.all_gather(dy_part, "mp", axis=1, tiled=True)
        picked = dy_full.reshape(step_tok, row_blocks, side)[:, out_blocks]
        d_act = jnp.einsum("tjkc,jkbc->tjb", picked, w_out, preferred_element_type=jnp.float32)
        _, pullback = jax.vjp(jax.nn.gelu, pre)
        d_pre = pullback(d_act)[0].astype(jnp.bfloat16)
        grad_out = grad_out + jnp.einsum(
            "tjb,tjkc->jkbc", act, picked, preferred_element_type=jnp.float32
        )
        grad_in = grad_in + jnp.einsum(
            "tjkb,tjc->jkbc", selected, d_pre, preferred_element_type=jnp.float32
        )
        back = jnp.einsum("tjc,jkbc->tjkb", d_pre, w_in, preferred_element_type=jnp.float32)
        partial_back = place_blocks(back, in_blocks, row_blocks)
        backs.append(
            lax.psum_scatter(
                partial_back.astype(jnp.bfloat16), "mp", scatter_dimension=1, tiled=True
            )
        )
    scale = 1.0 / math.sqrt(total_tok * lax.axis_size("dp"))
    in_share, out_share = (
        lax.psum_scatter(
            grad_in.astype(jnp.bfloat16), "dp", scatter_dimension=2, tiled=True
        ).astype(jnp.float32),
        lax.psum_scatter(
            grad_out.astype(jnp.bfloat16), "dp", scatter_dimension=2, tiled=True
        ).astype(jnp.float32),
    )
    output = jnp.concatenate(outputs, axis=0)
    grad_tokens = jnp.concatenate(backs, axis=0)
    return (output, grad_tokens, in_share * scale, out_share * scale)


def flip(u, m):
    if m == 0:
        return u
    return u + m * (1 - 2 * ((u // m) % 2))


def dot(a, b, dims):
    return lax.dot_general(a, b, (dims, ((), ())), preferred_element_type=jnp.float32)


def fused_kernel(dims, idx, x_hbm, dy_hbm, win_hbm, wout_hbm, out_hbm, back_hbm, red, *scratch):
    ndp, nmp, hb, side, own, tok, rows = dims
    fulls = [scratch[a * NQ : (a + 1) * NQ] for a in range(2)]
    (
        xg, xall, act, dpre, acth, dpreh, mine, theirs, arrived, wall, crecv,
        own_sem, y_send, y_recv, c_send, c_recv, f_send, f_recv, za_send, zb_send, b_send,
        za_recv, zb_recv, b_recv, fa_send, fa_recv, fb_send, fb_recv, go_sem, w_sem,
        free_sem, o_send, o_recv, p_send, p_recv, out_sem, g_send, g_recv, x_send, x_recv, r_send, r_recv, rl_sem,
    ) = scratch[2 * NQ :]
    nz = ndp // 2
    tc = tok // NQ
    blocks = own * nmp
    dp = lax.axis_index("dp")
    mp = lax.axis_index("mp")
    z, x = dp // 2, dp % 2
    y, core = mp // 2, mp % 2
    other_core = (dp, y * 2 + 1 - core)
    other_y = (dp, (1 - y) * 2 + core)
    other_x = (z * 2 + 1 - x, mp)
    g_core = other_core[1]
    g_y = other_y[1]
    g_far = (1 - y) * 2 + 1 - core
    heavy = core == z // 2
    hbase = (z % 2) * GROUP
    srcs = (x_hbm, dy_hbm)
    outs = (out_hbm, back_hbm)

    barrier = pltpu.get_barrier_semaphore()
    peers = [other_core, other_y, other_x] + [((dp + 2 * dz) % ndp, mp) for dz in range(1, nz)]
    for peer in peers:
        pl.semaphore_signal(barrier, inc=1, device_id=peer, device_id_type=MESH)
    pl.semaphore_wait(barrier, len(peers))

    def remote(src, dst, ssem, rsem, peer):
        return pltpu.make_async_remote_copy(
            src_ref=src, dst_ref=dst, send_sem=ssem, recv_sem=rsem,
            device_id=peer, device_id_type=MESH,
        )

    def lanes(i):
        return pl.ds(pl.multiple_of(i * side, side), side)

    def rows_at(base, n):
        return pl.ds(pl.multiple_of(base, tc), n)

    def held(a, q, slot):
        return fulls[a][q].at[pl.ds(slot * own, own)]

    def piece(a, q, i):
        return srcs[a].at[pl.ds(q * tc, tc), lanes(i)]

    def to_y(a, q, src, dst):
        return remote(src, dst, y_send.at[a, q], y_recv.at[a, q], other_y)

    def to_core(a, q, src, dst):
        return remote(src, dst, c_send.at[a, q], c_recv.at[a, q], other_core)

    def keep(a, q, src, dst):
        return pltpu.make_async_copy(src, dst, own_sem.at[a, q])

    def landed(send, a, q, slot):
        return send(a, q, held(a, q, slot), held(a, q, slot))

    def forward(a, q, slot):
        return remote(held(a, q, g_y), held(a, q, slot), f_send.at[a, q], f_recv.at[a, q], other_core)

    def weights():
        return (
            pltpu.make_async_copy(win_hbm, wall.at[0], w_sem.at[0]),
            pltpu.make_async_copy(wout_hbm, wall.at[1], w_sem.at[1]),
        )

    def loop(n, body, first=0):
        lax.fori_loop(first, n, lambda i, c: (body(i), c)[1], 0)

    def hold(a, q):
        def start(i):
            keep(a, q, piece(a, q, i), fulls[a][q].at[mp * own + i]).start()

        loop(own, start)

    def send_first(a):
        def start(i):
            to_y(a, 0, piece(a, 0, i), fulls[a][0].at[mp * own + i]).start()

        loop(own, start)

    def send_all(a, lead):
        if lead:
            send_first(a)
        for q in range(NQ):
            hold(a, q)
        for q in range(NQ):
            landed(keep, a, q, mp).wait()
            if q or not lead:
                landed(to_y, a, q, mp).start()
            landed(to_core, a, q, mp).start()

    for a in range(2):
        @pl.when(y != a)
        def _(a=a):
            send_all(a, True)
            send_all(1 - a, False)

    for cp in weights():
        cp.start()

    def z_rows(slot, q):
        return rows_at((q * nz + slot) * tc, tc)

    def size(spans):
        return sum(n for _, n in spans)

    def z_span(a, b, slot, q, at, n, ssem, rsem):
        return remote(
            xg.at[a, pl.ds(b * GROUP + at, n), pl.ds(q * tc, tc)],
            xall.at[a, pl.ds(at, n), z_rows(slot, q)],
            ssem.at[b, q], rsem.at[q], ((2 * core + b) * 2 + x, mp),
        )

    def near_rows(q, first=1):
        return pl.ds((q * nz + first) * tc, (nz - first) * tc)

    def to_groups(a, q, spans, ssem, rsem):
        for b in range(2):
            @pl.when(2 * core + b != z)
            def _(b=b):
                for at, n in spans:
                    z_span(a, b, (z - 2 * core - b + nz) % nz, q, at, n, ssem, rsem).start()

    def z_sent(a, b, q, n, ssem, rsem):
        z_span(a, b, 0, q, 0, n, ssem, rsem).wait_send()

    def near_part(a, q, at, n, ssem, rsem):
        part = xall.at[a, pl.ds(at, n), near_rows(q)]
        return remote(part, part, ssem.at[q], rsem.at[q], other_y)

    def pass_on(q, spans, here, ssem, rsem, held_spans):
        @pl.when(heavy)
        def _():
            near_part(y, q, 0, size(held_spans), ssem, here).wait_recv()
            for at, n in spans:
                near_part(y, q, at, n, ssem, rsem).start()

    def pass_lead(q):
        pass_on(q, LEAD, za_recv, fa_send, fa_recv, LEAD)

    def pass_rest(q):
        pass_on(q, RELAYS[q], zb_recv, fb_send, fb_recv, REST)

    def gather(a, q):
        landed(to_y, a, q, g_y).wait_recv()
        forward(a, q, g_y).start()
        landed(to_core, a, q, g_core).wait_recv()
        forward(a, q, g_far).wait_recv()

        def pack(i):
            xg[a, i, pl.ds(q * tc, tc)] = fulls[a][q][idx[a, i]]

        loop(hb, pack)

        @pl.when(heavy)
        def _():
            def own_rows(r):
                xall[a, r, z_rows(0, q)] = xg[a, hbase + r, pl.ds(q * tc, tc)]

            loop(GROUP, own_rows)

    def hidden_math(xs, dys, j):
        wi = wall[0, j].reshape(len(MASKS) * side, side)
        wo = jnp.concatenate([wall[1, j, k] for k in range(len(MASKS))], axis=1)
        pre = dot(jnp.concatenate(xs, axis=1), wi, ((1,), (0,)))
        d_act = dot(jnp.concatenate(dys, axis=1), wo, ((1,), (1,)))
        sq = pre * pre
        th = jnp.tanh(pre * (C0 + (C0 * C1) * sq))
        half = 0.5 + 0.5 * th
        value = pre * half
        slope = half + value * (1.0 - th) * (C0 + (3.0 * C0 * C1) * sq)
        return value.astype(jnp.bfloat16), (d_act * slope).astype(jnp.bfloat16)

    ht = tok // HALVES
    per = NQ // HALVES

    def hidden(h, first=0, last=hb):
        at = pl.ds(h * ht, ht)

        def one(j):
            act[j, at], dpre[j, at] = hidden_math(
                [xg[0, flip(j, m), at] for m in MASKS], [xg[1, flip(j, m), at] for m in MASKS], j
            )

        loop(last, one, first)

    def place(u):
        vs = [flip(u, m) for m in MASKS]
        wo = jnp.concatenate([wall[1, v, k] for k, v in enumerate(vs)], axis=0)
        wi = jnp.concatenate([wall[0, v, k] for k, v in enumerate(vs)], axis=1)
        out = dot(jnp.concatenate([act[v] for v in vs], axis=1), wo, ((1,), (0,)))
        back = dot(jnp.concatenate([dpre[v] for v in vs], axis=1), wi, ((1,), (1,)))
        for a, value in ((0, out), (1, back)):
            value = value.astype(jnp.bfloat16)
            for q in range(NQ):
                fulls[a][q][u] = value[q * tc : (q + 1) * tc]

    tables = (1, 0)

    def swap(a, q):
        return remote(
            fulls[a][q].at[pl.ds(hb, hb)], crecv.at[a, :, pl.ds(q * tc, tc)],
            o_send.at[a, q], o_recv.at[a, q], other_core,
        )

    def clear(h):
        for q in range(h * per, (h + 1) * per):
            for a in range(2):
                forward(a, q, g_y).wait_send()
                landed(to_y, a, q, mp).wait_send()
                landed(to_core, a, q, mp).wait_send()
                fulls[a][q][blocks] = jnp.zeros((tc, side), jnp.bfloat16)

    def hand_over(h):
        for a in range(2):
            for q in range(h * per, (h + 1) * per):
                for yy in range(2):
                    def fill(i, a=a, yy=yy, q=q):
                        fulls[a][q][hb + yy * own + i] = fulls[a][q][
                            idx[tables[a], hb + (2 * yy + 1 - core) * own + i]
                        ]
                    loop(own, fill)
                swap(a, q).start()

    def to_part(a, h):
        at = pl.ds(h * ht, ht)
        return remote(
            crecv.at[a, pl.ds((1 - y) * own, own), at], xg.at[a, pl.ds(0, own), at],
            p_send, p_recv.at[h], other_y,
        )

    def put(a, h, i):
        at = pl.ds(h * ht, ht)
        return pltpu.make_async_copy(crecv.at[a, y * own + i, at], outs[a].at[at, lanes(i)], out_sem)

    def finish(h):
        at = pl.ds(h * ht, ht)
        part = xg.at[:, pl.ds(0, own), at]
        remote(part, part, p_send, p_recv.at[h], other_y).wait_recv()
        for a in range(2):
            def one(i, a=a):
                crecv[a, y * own + i, at] = (
                    crecv[a, y * own + i, at].astype(jnp.float32) + xg[a, i, at].astype(jnp.float32)
                ).astype(jnp.bfloat16)
                put(a, h, i).start()

            loop(own, one)

    def merge(h):
        for a in range(2):
            for q in range(h * per, (h + 1) * per):
                swap(a, q).wait_recv()
                at = pl.ds(q * tc, tc)
                for yy in range(2):
                    def join(i, a=a, yy=yy, q=q, at=at):
                        crecv[a, yy * own + i, at] = crecv[a, yy * own + i, at] + fulls[a][q][
                            idx[tables[a], hb + (2 * yy + core) * own + i]
                        ]
                    loop(own, join)

    def emit(h):
        pl.semaphore_wait(free_sem.at[h], 1)
        for a in range(2):
            to_part(a, h).start()

    def near(r, p):
        at = pl.ds(pl.multiple_of(p * per * nz * tc, per * nz * tc), per * nz * tc)
        acth[r, at], dpreh[r, at] = hidden_math(
            [xall[0, flip(r, m), at] for m in MASKS], [xall[1, flip(r, m), at] for m in MASKS], hbase + r
        )

    def release(h):
        for q in range(h * per, (h + 1) * per):
            for b in range(2):
                @pl.when(2 * core + b != z)
                def _(b=b, q=q):
                    z_sent(y, b, q, size(LEAD), za_send, za_recv)
                    z_sent(y, b, q, size(REST), zb_send, zb_recv)
                    z_sent(1 - y, b, q, BOTHS[q][1], b_send, b_recv)

        pl.semaphore_signal(free_sem.at[h], inc=1, device_id=other_y, device_id_type=MESH)

    for q in range(NQ):
        for a in range(2):
            @pl.when(y == a)
            def _(a=a, q=q):
                gather(a, q)

        to_groups(y, q, LEAD, za_send, za_recv)
    for q in range(NQ):
        to_groups(y, q, REST, zb_send, zb_recv)
    for cp in weights():
        cp.wait()
    for q in range(NQ):
        for a in range(2):
            @pl.when(y != a)
            def _(a=a, q=q):
                gather(a, q)

        to_groups(1 - y, q, (BOTHS[q],), b_send, b_recv)
        if q == per - 1:
            hidden(0)
        if q == per:
            pass_lead(0)
            pass_lead(1)
    for q in range(per, NQ):
        pass_lead(q)
    hidden(1)
    clear(0)
    clear(1)
    loop(hb, place)
    hand_over(0)
    hand_over(1)
    for q in range(NQ):
        pass_rest(q)

    nk = len(MASKS)

    def to_x(r, a, k=0, n=nk):
        ssem, rsem = (x_send, x_recv) if k else (g_send.at[r % SLOTS, a], g_recv.at[r, a])
        at = pl.ds(k, n)
        return remote(theirs.at[r % SLOTS, a, at], arrived.at[r, a, at], ssem, rsem, other_x)

    def to_z(r, a, zd, b, at):
        return remote(
            mine.at[r, a, at, zd], red.at[a, b * GROUP + r, at], r_send, r_recv.at[b], (zd * 2 + x, mp)
        )

    def settle(r, a, k=0, n=nk):
        to_x(r, a, k, n).wait_recv()
        at = pl.ds(k, n)
        mine[r, a, at] = (
            mine[r, a, at].astype(jnp.float32) + arrived[r, a, at].astype(jnp.float32)
        ).astype(jnp.bfloat16)
        for dz in (2, 1, 3):
            to_z(r, a, (z + dz) % nz, z % 2, at).start()
        pltpu.make_async_copy(mine.at[r, a, at, z], red.at[a, hbase + r, at], rl_sem).start()

    def step(r, a, first=0, n=nk):
        for k in range(first, first + n):
            block = flip(r, MASKS[k])
            if a == 0:
                value = dot(xall[0, block], dpreh[r], ((0,), (0,)))
            else:
                value = dot(acth[r], xall[1, block], ((0,), (0,)))
            value = value.astype(jnp.bfloat16).reshape(nz, 2, rows, side)
            low, high = value[:, 0], value[:, 1]
            mine[r, a, k] = jnp.where(x == 0, low, high)
            theirs[r % SLOTS, a, k] = jnp.where(x == 0, high, low)
        to_x(r, a, first, n).start()

    @pl.when(heavy)
    def _():
        def grads(r):
            for a in range(2):
                @pl.when(r >= SLOTS)
                def _(a=a):
                    to_x(r - SLOTS, a).wait_send()

                step(r, a)

                @pl.when(r > 0)
                def _(a=a):
                    settle(r - 1, a)

        def both_steps(r):
            loop(HALVES, functools.partial(near, r))
            grads(r)

        def landed_in(h, counts, ssem, rsem):
            for q in range(h * per, (h + 1) * per):
                near_part(1 - y, q, 0, counts[q], ssem, rsem).wait_recv()

        for h in range(HALVES):
            landed_in(h, [size(LEAD)] * NQ, fa_send, fa_recv)
            near(0, h)
        grads(0)
        release(0)
        release(1)
        merge(0)
        merge(1)
        pl.semaphore_signal(go_sem, inc=1, device_id=other_core, device_id_type=MESH)
        emit(0)
        emit(1)
        for h in range(HALVES):
            landed_in(h, [size(spans) for spans in RELAYS], fb_send, fb_recv)
            landed_in(h, [n for _, n in BOTHS], fb_send, b_recv)
            near(1, h)
        grads(1)
        loop(6, both_steps, 2)
        finish(0)
        loop(GROUP - 1, both_steps, 6)
        last = GROUP - 1
        loop(HALVES, functools.partial(near, last))
        to_x(last - SLOTS, 0).wait_send()
        to_x(last - SLOTS, 1).wait_send()
        step(last, 0)
        settle(last - 1, 0)
        step(last, 1, 0, 2)
        settle(last - 1, 1)
        step(last, 1, 2, 2)
        settle(last, 0)
        settle(last, 1, 0, 2)
        settle(last, 1, 2, 2)

    @pl.when(jnp.logical_not(heavy))
    def _():
        release(0)
        release(1)
        merge(0)
        merge(1)
        pl.semaphore_wait(go_sem, 1)
        emit(0)
        emit(1)
        finish(0)

    finish(1)

    for q in range(NQ):
        for a in range(2):
            swap(a, q).wait_send()

        @pl.when(heavy)
        def _(q=q):
            near_part(y, q, 0, size(LEAD), fa_send, fa_recv).wait_send()
            near_part(y, q, 0, size(RELAYS[q]), fb_send, fb_recv).wait_send()

    remote(crecv.at[0], crecv.at[0], p_send, p_recv.at[0], other_y).wait_send()
    pltpu.make_async_copy(crecv.at[0], crecv.at[0], out_sem).wait()

    @pl.when(heavy)
    def _():
        for r in range(GROUP - SLOTS, GROUP):
            for a in range(2):
                if a == 0 or r < GROUP - 1:
                    to_x(r, a).wait_send()
        to_x(GROUP - 1, 1, 0, 2).wait_send()
        to_x(GROUP - 1, 1, 2, 2).wait_send()
        group = red.at[:, pl.ds(hbase, GROUP)]
        pltpu.make_async_copy(group, group, rl_sem).wait()
        sent = mine.at[pl.ds(0, GROUP * (nz - 1) // nz)]
        remote(sent, sent, r_send, r_recv.at[0], other_x).wait_send()

    for b in range(2):
        @pl.when(2 * core + b != z)
        def _(b=b):
            got = red.at[:, pl.ds(b * GROUP, GROUP)]
            remote(got, got, r_send, r_recv.at[b], other_x).wait_recv()


def write_kernel(
    scale, out_hbm, back_hbm, red, out, back, grad_in, grad_out, kept, low, high, k_in, k_out, r_in, r_out
):
    n = red.shape[1] // PIECES
    srcs, dsts, grads = (out_hbm, back_hbm), (out, back), (grad_in, grad_out)

    def load(a, p):
        at = pl.ds(p * n, n)
        return pltpu.make_async_copy(red.at[a, at], low.at[a, at], r_in.at[a, p])

    def save(a, p):
        at = pl.ds(p * n, n)
        return pltpu.make_async_copy(high.at[a, at], grads[a].at[at], r_out.at[a, p])

    def take(a):
        return pltpu.make_async_copy(srcs[a], kept.at[a], k_in.at[a])

    def give(a):
        return pltpu.make_async_copy(kept.at[a], dsts[a], k_out.at[a])

    for p in range(PIECES):
        for a in range(2):
            load(a, p).start()
    for a in range(2):
        take(a).start()
    for p in range(PIECES):
        for a in range(2):
            load(a, p).wait()
            at = pl.ds(p * n, n)
            high[a, at] = low[a, at].astype(jnp.float32) * scale
            save(a, p).start()
    for a in range(2):
        take(a).wait()
        give(a).start()
    for a in range(2):
        for p in range(PIECES):
            save(a, p).wait()
        give(a).wait()


def shards_fused(ndp, nmp, tokens, cotangent, w_in, w_out, in_blocks, out_blocks):
    hb, kk, side, _ = w_in.shape
    tok, feats = tokens.shape
    own = feats // side
    blocks = own * nmp
    nz = ndp // 2
    rows = side // ndp
    tc = tok // NQ
    first = jnp.stack([in_blocks[:, 0], out_blocks[:, 0]])
    place = jnp.arange(hb, dtype=jnp.int32)[:, None]
    hit = first[:, :, None] == jnp.arange(blocks, dtype=jnp.int32)
    table = jnp.concatenate([first, jnp.min(jnp.where(hit, place, blocks), axis=1)], axis=1)
    bf = jnp.bfloat16
    any_spec = pl.BlockSpec(memory_space=pl.ANY)
    smem = pl.BlockSpec(memory_space=pltpu.SMEM)
    dma = pltpu.SemaphoreType.DMA
    output, grad_tokens, red = pl.pallas_call(
        functools.partial(fused_kernel, (ndp, nmp, hb, side, own, tok, rows)),
        out_shape=(
            jax.ShapeDtypeStruct((tok, feats), bf),
            jax.ShapeDtypeStruct((tok, feats), bf),
            jax.ShapeDtypeStruct((2, hb, kk, rows, side), bf),
        ),
        in_specs=[smem] + [any_spec] * 4,
        out_specs=(any_spec,) * 3,
        scratch_shapes=[pltpu.VMEM((blocks + 1, tc, side), bf)] * (2 * NQ)
        + [
            pltpu.VMEM((2, hb, tok, side), bf),
            pltpu.VMEM((2, GROUP, nz * tok, side), bf),
            pltpu.VMEM((hb, tok, side), bf),
            pltpu.VMEM((hb, tok, side), bf),
            pltpu.VMEM((GROUP, nz * tok, side), bf),
            pltpu.VMEM((GROUP, nz * tok, side), bf),
            pltpu.VMEM((GROUP, 2, kk, nz, rows, side), bf),
            pltpu.VMEM((SLOTS, 2, kk, nz, rows, side), bf),
            pltpu.VMEM((GROUP, 2, kk, nz, rows, side), bf),
            pltpu.VMEM((2, hb, kk, side, side), bf),
            pltpu.VMEM((2, hb, tok, side), bf),
        ]
        + [dma((2, NQ))] * 10
        + [dma((NQ,))] * 7
        + [pltpu.SemaphoreType.REGULAR, dma((2,)), pltpu.SemaphoreType.REGULAR((2,))]
        + [dma((2, NQ))] * 2
        + [dma, dma((2,)), dma]
        + [dma((SLOTS, 2)), dma((GROUP, 2))]
        + [dma, dma, dma, dma((2,)), dma],
        compiler_params=pltpu.CompilerParams(
            collective_id=0, has_side_effects=True, vmem_limit_bytes=67_000_000
        ),
    )(
        table,
        tokens, cotangent, w_in, w_out,
    )
    scale = 1.0 / math.sqrt(tok * ndp)
    wide = jnp.float32
    return pl.pallas_call(
        functools.partial(write_kernel, scale),
        out_shape=(
            jax.ShapeDtypeStruct((tok, feats), bf),
            jax.ShapeDtypeStruct((tok, feats), bf),
            jax.ShapeDtypeStruct((hb, kk, rows, side), wide),
            jax.ShapeDtypeStruct((hb, kk, rows, side), wide),
        ),
        in_specs=[any_spec] * 3,
        out_specs=(any_spec,) * 4,
        scratch_shapes=[
            pltpu.VMEM((2, tok, feats), bf),
            pltpu.VMEM((2, hb, kk, rows, side), bf),
            pltpu.VMEM((2, hb, kk, rows, side), wide),
            dma((2,)), dma((2,)), dma((2, PIECES)), dma((2, PIECES)),
        ],
        compiler_params=pltpu.CompilerParams(vmem_limit_bytes=67_000_000),
    )(output, grad_tokens, red)


def solution(mesh):
    ndp, nmp = mesh.shape["dp"], mesh.shape["mp"]

    def shards(tokens, cotangent, w_in, w_out, in_blocks, out_blocks):
        hb, kk, side, _ = w_in.shape
        blocks = tokens.shape[1] * nmp // side
        fits = (
            nmp == 4
            and kk == len(MASKS)
            and ndp == 2 * nmp
            and blocks == GROUP * nmp
            and 2 * hb == blocks
            and tokens.shape[0] % (16 * NQ) == 0
            and side % (16 * ndp) == 0
        )
        args = (tokens, cotangent, w_in, w_out, in_blocks, out_blocks)
        if fits:
            return shards_fused(ndp, nmp, *args)
        return shards_plain(*args)

    placed = (
        P("dp", "mp"),
        P("dp", "mp"),
        P("mp", None, None, None),
        P("mp", None, None, None),
        P("mp", None),
        P("mp", None),
    )
    return jax.shard_map(
        shards,
        mesh=mesh,
        in_specs=placed,
        out_specs=(
            P("dp", "mp"),
            P("dp", "mp"),
            P("mp", None, "dp", None),
            P("mp", None, "dp", None),
        ),
        check_vma=False,
    )
```
